512 devices in a mesh: rows: 64 (over y, z), cols: 8 (over x, core).
Axes of the slice: x: 4, y: 4, z: 16, core: 2. Of those that a mesh axis runs over, the one named last changes fastest.
Arguments:
- node_features: bfloat16 [65536, 512], P('rows', 'cols'), may hold values from -6 to 6
- weight: bfloat16 [512, 512], replicated, may hold values from -0.25 to 0.25
- tile_values: bfloat16 [4096, 128, 128], P('rows'), may hold values from -0.1875 to 0.1875
- tile_row: int32 [4096], P('rows'), may hold values from 0 to 7
- source_owner: int32 [4096, 1], P('rows'), may hold values from 0 to 63; in each aligned block of 64 rows (0 to 63, 64 to 127, ...) at most 2 rows name the same one
- source_block: int32 [4096], P('rows'), may hold values from 0 to 7
- labels: int32 [65536], P('rows'), may hold values from 0 to 511
Outputs:
- activations: bfloat16 [65536, 512], P('rows', 'cols')
- weight_grad: float32 [512, 512], P(None, 'cols')
- feature_grad: bfloat16 [65536, 512], P('rows', 'cols')
The draws below stay inside these ranges and needn't reach their ends.
Inputs may be any that keep to these rules, and one draw needn't show every extreme that they name: `source_owner`: of the 64 tiles of one index of rows, at most 2 name the same owner.
All inputs are finite; a program needn't handle non-finite values.
Results may differ from the reference program's by a relative error of at most 0.0095.
Values may be sent and summed in bfloat16 or wider, within the bound.
A program may use at most 64 MiB of HBM per device.

```python
import math
import jax
import jax.numpy as jnp
import numpy as np
from jax import lax

F = 512
BLK = 128
NB_DEV = 8
TILES_DEV = 64
CAP = 2
TILES = 4096
NBLK = 512
NODES = 65536
N_ROWS = 64


def touch_ends(entries, key, least, top_value):
    spot = [jax.random.randint(jax.random.fold_in(key, axis), (), 0, length) for axis, length in enumerate(entries.shape)]
    longest = entries.shape.index(max(entries.shape))
    neighbour = spot[:longest] + [(spot[longest] + 1) % entries.shape[longest]] + spot[longest + 1:]
    return entries.at[tuple(spot)].set(least).at[tuple(neighbour)].set(top_value)


def shard_levels(rng, shape, shards, low, largest):
    loudness, own = 1.0, jax.random.fold_in(rng, 6)
    for axis_at, blocks in shards:
        steps = jnp.exp(jax.random.uniform(jax.random.fold_in(own, axis_at), (blocks,), jnp.float32, low / len(shards), largest / len(shards)))
        loudness = loudness * jnp.repeat(steps, shape[axis_at] // blocks).reshape([-1 if axis == axis_at else 1 for axis in range(len(shape))])
    return loudness


def shared_out(own_key, own, number, rows, number_of, top, limit, lean):
    order = jax.random.permutation(own_key, number_of)
    crowded, usual = portions_of(number_of, rows * top, limit, lean, True), portions_of(number_of, rows * top, limit, lean, False)
    places = jnp.arange(number_of)

    def named(lengths, offset_by):
        used = int((lengths > 0).sum())
        fixed = max(1, used // 4)
        shifted = fixed + (places - fixed + offset_by * (used - fixed)) % max(1, number_of - fixed)
        return jnp.zeros((number_of,), jnp.int32).at[order[jnp.where(places < fixed, places, shifted)]].set(jnp.asarray(lengths, jnp.int32))

    lengths = jnp.where(number % 4 == 0, named(crowded, number // 4), named(usual, number - number // 4 - 1))
    mixed = jax.random.permutation(jax.random.fold_in(own, 3), number_of)
    donor, sink = mixed[0:number_of // 2 * 2:2], mixed[1:number_of // 2 * 2:2]
    slack = jnp.minimum(lengths[donor] - 1, limit - lengths[sink]) // 2
    slack = jnp.where((donor == order[0]) | (sink == order[0]) | (lengths[sink] == 0), 0, jnp.maximum(slack, 0))
    shifted = jax.random.randint(jax.random.fold_in(own, 4), (number_of // 2,), 0, 1 << 20) % (slack + 1)
    lengths = lengths.at[donor].add(-shifted).at[sink].add(shifted)
    members = jnp.searchsorted(jnp.cumsum(lengths), jnp.arange(rows * top), side="right").astype(jnp.int32)
    table = members.reshape(top, rows).T
    table = table[jax.random.permutation(jax.random.fold_in(own, 1), rows)]
    offset_by = jax.random.randint(jax.random.fold_in(own, 2), (rows, 1), 0, top)
    return jnp.take_along_axis(table, (jnp.arange(top)[None, :] + offset_by) % top, axis=1)


def portions_of(count, total, most, skew, full):
    portions = [(1 << 20) // math.isqrt(standing ** skew) + 1 for standing in range(1, count + 1)]
    largest = most if full else min(most, max(-(-total // count), total * portions[0] // sum(portions)))
    least = 1 if total - largest >= count - 1 else 0
    given, surplus = [largest] + [least] * (count - 1), total - largest - least * (count - 1)
    while surplus > 0:
        free = [i for i in range(1, count) if given[i] < largest] or [i for i in range(1, count) if given[i] < most]
        pool, left = sum([portions[i] for i in free]), surplus
        for i in free:
            addition = min(most - given[i], max(1, left * portions[i] // pool), surplus)
            given[i] = given[i] + addition
            surplus = surplus - addition
    return np.array(given)


def gaussian(own_key, extent, width, most, pieces=(), kind=jnp.bfloat16):
    values = width * jax.random.normal(own_key, extent, jnp.float32)
    if pieces:
        values = values * shard_levels(own_key, extent, pieces, -0.22, 0.18)
    return jnp.clip(values, -most, most).astype(kind)


def setup_inputs(seed: int = 0) -> dict:
    seeds = jax.random.split(jax.random.key(seed), 8)
    node_features = gaussian(seeds[0], (NODES, F), 1.0, 6.0, ((0, 64), (1, 8)))
    weight = gaussian(seeds[1], (F, F), F ** -0.5, 0.25)
    tile_values = gaussian(seeds[2], (TILES, BLK, BLK), (BLK * TILES_DEV // NB_DEV) ** -0.5, 0.1875, ((0, 64),))
    tile_row = touch_ends(jax.random.randint(seeds[3], (TILES,), 0, NB_DEV), jax.random.fold_in(seeds[3], 1), 0, NB_DEV - 1).astype(jnp.int32)
    source_owner_keys = jax.random.split(jax.random.fold_in(seeds[4], 1), TILES // TILES_DEV)
    source_owner_turns = jax.random.permutation(jax.random.fold_in(seeds[4], 3), TILES // TILES_DEV)
    source_owner = jax.vmap(lambda own, number: shared_out(jax.random.fold_in(seeds[4], 2), own, number, TILES_DEV, N_ROWS, 1, CAP, 2))(source_owner_keys, source_owner_turns).reshape((TILES, 1))
    source_block = touch_ends(jax.random.randint(seeds[5], (TILES,), 0, NB_DEV), jax.random.fold_in(seeds[5], 1), 0, NB_DEV - 1).astype(jnp.int32)
    labels = touch_ends(jax.random.randint(seeds[6], (NODES,), 0, F), jax.random.fold_in(seeds[6], 1), 0, F - 1).astype(jnp.int32)
    return {"node_features": node_features, "weight": weight, "tile_values": tile_values, "tile_row": tile_row, "source_owner": source_owner, "source_block": source_block, "labels": labels}


def reference(node_features, weight, tile_values, tile_row, source_owner, source_block, labels):
    feature_blocks = node_features.reshape(NBLK, BLK, F)
    device_ids = jnp.arange(N_ROWS, dtype=jnp.int32)
    block_ids = jnp.arange(NB_DEV, dtype=jnp.int32)
    tiles_grouped = tile_values.reshape(N_ROWS, TILES_DEV, BLK, BLK)
    rows_grouped = tile_row.astype(jnp.int32).reshape(N_ROWS, TILES_DEV)
    cols_grouped = (source_owner[:, 0] * NB_DEV + source_block).astype(jnp.int32).reshape(N_ROWS, TILES_DEV)

    def aggregate(group_data):
        tile_block, rows_here, cols_here = group_data
        gathered = feature_blocks[cols_here].astype(jnp.float32)
        products = jnp.einsum('tij,tjf->tif', tile_block.astype(jnp.float32), gathered, precision=lax.Precision.HIGHEST)
        onehot = (rows_here[:, None] == block_ids[None, :]).astype(jnp.float32)
        return jnp.einsum('tb,tif->bif', onehot, products, precision=lax.Precision.HIGHEST)
    summed = lax.map(aggregate, (tiles_grouped, rows_grouped, cols_grouped))
    aggregated = summed.reshape(NODES, F).astype(jnp.bfloat16)
    hidden = jnp.dot(aggregated, weight, preferred_element_type=jnp.float32)
    sigmoid = jax.nn.sigmoid(hidden)
    activated = hidden * sigmoid
    slopes = sigmoid * (1.0 + hidden * (1.0 - sigmoid))
    target = (labels[:, None] == jnp.arange(F, dtype=jnp.int32)[None, :]).astype(jnp.float32)
    out_grad = ((activated - target) * slopes).astype(jnp.bfloat16)
    weight_grad = jnp.dot(aggregated.T, out_grad, preferred_element_type=jnp.float32) / math.sqrt(NODES)
    agg_grad = jnp.dot(out_grad, weight.T, preferred_element_type=jnp.float32).astype(jnp.bfloat16)
    grad_blocks = agg_grad.reshape(NBLK, BLK, F)

    def spread(running, group_data):
        tile_block, rows_here, cols_here, device = group_data
        sources = grad_blocks[device * NB_DEV + rows_here].astype(jnp.float32)
        tile_terms = jnp.einsum('tji,tjf->tif', tile_block.astype(jnp.float32), sources, precision=lax.Precision.HIGHEST)
        return (running.at[cols_here].add(tile_terms), None)
    grad_total, unused = lax.scan(spread, jnp.zeros((NBLK, BLK, F), jnp.float32), (tiles_grouped, rows_grouped, cols_grouped, device_ids))
    feature_grad = grad_total.reshape(NODES, F).astype(jnp.bfloat16)
    return (activated.astype(jnp.bfloat16), weight_grad, feature_grad)
```

```python
import math

import jax
import jax.numpy as jnp
from jax import lax
from jax.sharding import PartitionSpec as P


def slot_ranks(owners):
    positions = jnp.arange(owners.shape[0], dtype=jnp.int32)
    earlier = (owners[:, None] == owners[None, :]) & (positions[None, :] < positions[:, None])
    return jnp.sum(earlier.astype(jnp.int32), axis=1)


def row_all_reduce(partial):
    row_devices = lax.axis_size("rows")
    k, c = partial.shape
    pieces = partial.reshape(row_devices, k // row_devices, c)
    gathered = lax.all_to_all(pieces, "rows", split_axis=0, concat_axis=0, tiled=True)
    reduced = jnp.sum(gathered, axis=0)
    spread = jnp.broadcast_to(reduced[None], (row_devices,) + reduced.shape)
    return lax.all_to_all(spread, "rows", split_axis=0, concat_axis=0, tiled=True).reshape(k, c)


def per_device(node_features, weight, tile_values, tile_row, source_owner, source_block, labels):
    local_rows, col_width = node_features.shape
    block_size = tile_values.shape[1]
    local_blocks = local_rows // block_size
    row_devices = lax.axis_size("rows")
    capacity = 2 * tile_values.shape[0] // row_devices
    owners = source_owner[:, 0]
    slot_rank = slot_ranks(owners)
    local_ids = jnp.arange(local_blocks, dtype=jnp.int32)
    row_onehot = (tile_row[:, None] == local_ids[None, :]).astype(jnp.float32)
    request = jnp.zeros((row_devices, capacity), jnp.int32).at[owners, slot_rank].set(source_block)
    wanted = lax.all_to_all(request, "rows", split_axis=0, concat_axis=0, tiled=True)
    own_blocks = node_features.reshape(local_blocks, block_size, col_width)
    outgoing = own_blocks[wanted]
    incoming = lax.all_to_all(outgoing, "rows", split_axis=0, concat_axis=0, tiled=True)
    source_rows = incoming[owners, slot_rank]
    products = jnp.einsum(
        "tij,tjf->tif", tile_values, source_rows, preferred_element_type=jnp.float32
    )
    summed = jnp.einsum("tb,tif->bif", row_onehot, products, precision=lax.Precision.HIGHEST)
    aggregated = summed.reshape(local_rows, col_width).astype(jnp.bfloat16)
    aggregated_all = lax.all_gather(aggregated, "cols", axis=1, tiled=True)
    col_index = lax.axis_index("cols")
    w_columns = lax.dynamic_slice_in_dim(weight, col_index * col_width, col_width, 1)
    w_rows = lax.dynamic_slice_in_dim(weight, col_index * col_width, col_width, 0)
    hidden = jnp.dot(aggregated_all, w_columns, preferred_element_type=jnp.float32)
    sigmoid = jax.nn.sigmoid(hidden)
    activated = hidden * sigmoid
    slopes = sigmoid * (1.0 + hidden * (1.0 - sigmoid))
    feature_ids = col_index * col_width + jnp.arange(col_width, dtype=jnp.int32)
    target = (labels[:, None] == feature_ids[None, :]).astype(jnp.float32)
    out_grad = ((activated - target) * slopes).astype(jnp.bfloat16)
    grad_all = lax.all_gather(out_grad, "cols", axis=1, tiled=True)
    weight_terms = jnp.einsum(
        "nk,nc->kc", aggregated_all, out_grad, preferred_element_type=jnp.float32
    )
    node_total = local_rows * row_devices
    weight_grad = row_all_reduce(weight_terms) / math.sqrt(node_total)
    agg_grad = jnp.einsum("nc,kc->nk", grad_all, w_rows, preferred_element_type=jnp.float32).astype(
        jnp.bfloat16
    )
    grad_rows = agg_grad.reshape(local_blocks, block_size, col_width)[tile_row]
    sent_terms = jnp.einsum(
        "tji,tjf->tif", tile_values, grad_rows, preferred_element_type=jnp.float32
    )
    send_terms = (
        jnp.zeros((row_devices, capacity, block_size, col_width), jnp.bfloat16)
        .at[owners, slot_rank]
        .set(sent_terms.astype(jnp.bfloat16))
    )
    received = lax.all_to_all(send_terms, "rows", split_axis=0, concat_axis=0, tiled=True)
    placing = (wanted[:, :, None] == local_ids[None, None, :]).astype(jnp.float32)
    feature_grad = jnp.einsum(
        "scb,scif->bif", placing, received.astype(jnp.float32), precision=lax.Precision.HIGHEST
    ).reshape(local_rows, col_width)
    return (activated.astype(jnp.bfloat16), weight_grad, feature_grad.astype(jnp.bfloat16))


def solution(mesh):
    return jax.shard_map(
        per_device,
        mesh=mesh,
        in_specs=(
            P("rows", "cols"),
            P(),
            P("rows", None, None),
            P("rows"),
            P("rows", None),
            P("rows"),
            P("rows"),
        ),
        out_specs=(P("rows", "cols"), P(None, "cols"), P("rows", "cols")),
        check_vma=False,
    )
```

```python
import functools
import math

import jax
import jax.numpy as jnp
from jax import lax
from jax.experimental import pallas as pl
from jax.experimental.pallas import tpu as pltpu
from jax.sharding import PartitionSpec as P

MESH = pl.DeviceIdType.MESH


def _a2a_kernel(x_hbm, o_hbm, send_sems, recv_sems, local_sem):
    n = x_hbm.shape[0]
    me = lax.axis_index("rows")
    barrier = pltpu.get_barrier_semaphore()

    def greet(k, carry):
        peer = lax.rem(me + k, n)
        pl.semaphore_signal(barrier, 1, device_id={"rows": peer}, device_id_type=MESH)
        return carry

    lax.fori_loop(1, n, greet, 0)
    pl.semaphore_wait(barrier, n - 1)
    local = pltpu.make_async_copy(x_hbm.at[me], o_hbm.at[me], local_sem)
    local.start()

    def outgoing(peer):
        return pltpu.make_async_remote_copy(
            src_ref=x_hbm.at[peer], dst_ref=o_hbm.at[me], send_sem=send_sems.at[peer],
            recv_sem=recv_sems.at[me], device_id={"rows": peer}, device_id_type=MESH)

    def incoming(src):
        return pltpu.make_async_remote_copy(
            src_ref=x_hbm.at[src], dst_ref=o_hbm.at[src], send_sem=send_sems.at[src],
            recv_sem=recv_sems.at[src], device_id={"rows": src}, device_id_type=MESH)

    def start(k, carry):
        outgoing(lax.rem(me + k, n)).start()
        return carry

    lax.fori_loop(1, n, start, 0)

    def finish(k, carry):
        outgoing(lax.rem(me + k, n)).wait_send()
        incoming(lax.rem(me + n - k, n)).wait_recv()
        return carry

    lax.fori_loop(1, n, finish, 0)
    local.wait()


def rows_all_to_all(x, collective_id):
    n = x.shape[0]
    return pl.pallas_call(
        _a2a_kernel,
        out_shape=jax.ShapeDtypeStruct(x.shape, x.dtype),
        in_specs=[pl.BlockSpec(memory_space=pl.ANY)],
        out_specs=pl.BlockSpec(memory_space=pl.ANY),
        scratch_shapes=[
            pltpu.SemaphoreType.DMA((n,)),
            pltpu.SemaphoreType.DMA((n,)),
            pltpu.SemaphoreType.DMA(()),
        ],
        compiler_params=pltpu.CompilerParams(collective_id=collective_id, has_side_effects=True),
    )(x)


def slot_ranks(owners):
    positions = jnp.arange(owners.shape[0], dtype=jnp.int32)
    earlier = (owners[:, None] == owners[None, :]) & (positions[None, :] < positions[:, None])
    return jnp.sum(earlier.astype(jnp.int32), axis=1)


def row_all_reduce(partial):
    row_devices = lax.axis_size("rows")
    k, c = partial.shape
    pieces = partial.reshape(row_devices, k // row_devices, c)
    gathered = lax.all_to_all(pieces, "rows", split_axis=0, concat_axis=0, tiled=True)
    reduced = jnp.sum(gathered, axis=0)
    spread = jnp.broadcast_to(reduced[None], (row_devices,) + reduced.shape)
    return lax.all_to_all(spread, "rows", split_axis=0, concat_axis=0, tiled=True).reshape(k, c)


def per_device(node_features, weight, tile_values, tile_row, source_owner, source_block, labels):
    local_rows, col_width = node_features.shape
    block_size = tile_values.shape[1]
    local_blocks = local_rows // block_size
    row_devices = lax.axis_size("rows")
    capacity = 2 * tile_values.shape[0] // row_devices
    owners = source_owner[:, 0]
    slot_rank = slot_ranks(owners)
    local_ids = jnp.arange(local_blocks, dtype=jnp.int32)
    row_onehot = (tile_row[:, None] == local_ids[None, :]).astype(jnp.float32)
    request = jnp.zeros((row_devices, capacity), jnp.int32).at[owners, slot_rank].set(source_block)
    wanted = lax.all_to_all(request, "rows", split_axis=0, concat_axis=0, tiled=True)
    own_blocks = node_features.reshape(local_blocks, block_size, col_width)
    outgoing = own_blocks[wanted].reshape(row_devices, block_size, capacity * col_width)
    incoming = rows_all_to_all(outgoing, 0).reshape(row_devices, capacity, block_size, col_width)
    source_rows = incoming[owners, slot_rank]
    products = jnp.einsum(
        "tij,tjf->tif", tile_values, source_rows, preferred_element_type=jnp.float32
    )
    summed = jnp.einsum("tb,tif->bif", row_onehot, products, precision=lax.Precision.HIGHEST)
    aggregated = summed.reshape(local_rows, col_width).astype(jnp.bfloat16)
    aggregated_all = lax.all_gather(aggregated, "cols", axis=1, tiled=True)
    col_index = lax.axis_index("cols")
    w_columns = lax.dynamic_slice_in_dim(weight, col_index * col_width, col_width, 1)
    w_rows = lax.dynamic_slice_in_dim(weight, col_index * col_width, col_width, 0)
    hidden = jnp.dot(aggregated_all, w_columns, preferred_element_type=jnp.float32)
    sigmoid = jax.nn.sigmoid(hidden)
    activated = hidden * sigmoid
    slopes = sigmoid * (1.0 + hidden * (1.0 - sigmoid))
    feature_ids = col_index * col_width + jnp.arange(col_width, dtype=jnp.int32)
    target = (labels[:, None] == feature_ids[None, :]).astype(jnp.float32)
    out_grad = ((activated - target) * slopes).astype(jnp.bfloat16)
    grad_all = lax.all_gather(out_grad, "cols", axis=1, tiled=True)
    weight_terms = jnp.einsum(
        "nk,nc->kc", aggregated_all, out_grad, preferred_element_type=jnp.float32
    )
    node_total = local_rows * row_devices
    weight_grad = row_all_reduce(weight_terms) / math.sqrt(node_total)
    agg_grad = jnp.einsum("nc,kc->nk", grad_all, w_rows, preferred_element_type=jnp.float32).astype(
        jnp.bfloat16
    )
    grad_rows = agg_grad.reshape(local_blocks, block_size, col_width)[tile_row]
    sent_terms = jnp.einsum(
        "tji,tjf->tif", tile_values, grad_rows, preferred_element_type=jnp.float32
    )
    send_terms = (
        jnp.zeros((row_devices, capacity, block_size, col_width), jnp.bfloat16)
        .at[owners, slot_rank]
        .set(sent_terms.astype(jnp.bfloat16))
    )
    received = rows_all_to_all(
        send_terms.reshape(row_devices, block_size, capacity * col_width), 1
    ).reshape(row_devices, capacity, block_size, col_width)
    placing = (wanted[:, :, None] == local_ids[None, None, :]).astype(jnp.float32)
    feature_grad = jnp.einsum(
        "scb,scif->bif", placing, received.astype(jnp.float32), precision=lax.Precision.HIGHEST
    ).reshape(local_rows, col_width)
    return (activated.astype(jnp.bfloat16), weight_grad, feature_grad.astype(jnp.bfloat16))


def solution(mesh):
    return jax.shard_map(
        per_device,
        mesh=mesh,
        in_specs=(
            P("rows", "cols"),
            P(),
            P("rows", None, None),
            P("rows"),
            P("rows", None),
            P("rows"),
            P("rows"),
        ),
        out_specs=(P("rows", "cols"), P(None, "cols"), P("rows", "cols")),
        check_vma=False,
    )
```

```python
import math

import jax
import jax.numpy as jnp
from jax import lax
from jax.sharding import PartitionSpec as P


def slot_ranks(owners):
    positions = jnp.arange(owners.shape[0], dtype=jnp.int32)
    earlier = (owners[:, None] == owners[None, :]) & (positions[None, :] < positions[:, None])
    return jnp.sum(earlier.astype(jnp.int32), axis=1)


def rows_exchange(x):
    return lax.all_to_all(x, "rows", split_axis=0, concat_axis=0, tiled=True)


def row_all_reduce(partial):
    row_devices = lax.axis_size("rows")
    k, c = partial.shape
    pieces = partial.reshape(row_devices, k // row_devices, c)
    reduced = jnp.sum(rows_exchange(pieces), axis=0)
    spread = jnp.broadcast_to(reduced[None], (row_devices,) + reduced.shape)
    return rows_exchange(spread).reshape(k, c)


def per_device(node_features, weight, tile_values, tile_row, source_owner, source_block, labels):
    local_rows, col_width = node_features.shape
    block_size = tile_values.shape[1]
    local_blocks = local_rows // block_size
    row_devices = lax.axis_size("rows")
    col_devices = lax.axis_size("cols")
    tiles = tile_values.shape[0]
    capacity = 2 * tiles // row_devices
    half = col_width // 2
    owners = source_owner[:, 0]
    slot_rank = slot_ranks(owners)
    local_ids = jnp.arange(local_blocks, dtype=jnp.int32)
    row_onehot = (tile_row[:, None] == local_ids[None, :]).astype(jnp.float32)
    request = jnp.zeros((row_devices, capacity), jnp.int32).at[owners, slot_rank].set(source_block)
    wanted = rows_exchange(request)
    own_blocks = node_features.reshape(local_blocks, block_size, col_width)
    outgoing = own_blocks[wanted]
    col_index = lax.axis_index("cols")
    w_columns = lax.dynamic_slice_in_dim(weight, col_index * col_width, col_width, 1)
    w_rows = lax.dynamic_slice_in_dim(weight, col_index * col_width, col_width, 0)
    w_split = w_columns.reshape(col_devices, col_width, col_width)

    def aggregate(part):
        source_rows = part[owners, slot_rank]
        products = jnp.einsum(
            "tij,tjf->tif", tile_values, source_rows, preferred_element_type=jnp.float32
        )
        summed = jnp.einsum("tb,tif->bif", row_onehot, products, precision=lax.Precision.HIGHEST)
        return summed.reshape(local_rows, part.shape[-1]).astype(jnp.bfloat16)

    first = aggregate(rows_exchange(outgoing[..., :half]))
    second_out, first = lax.optimization_barrier((outgoing[..., half:], first))
    first_all = lax.all_gather(first, "cols", axis=0, tiled=False)
    second = aggregate(rows_exchange(second_out))
    second_all = lax.all_gather(second, "cols", axis=0, tiled=False)
    hidden = jnp.einsum(
        "jnf,jfc->nc", first_all, w_split[:, :half], preferred_element_type=jnp.float32
    ) + jnp.einsum(
        "jnf,jfc->nc", second_all, w_split[:, half:], preferred_element_type=jnp.float32
    )
    sigmoid = jax.nn.sigmoid(hidden)
    activated = hidden * sigmoid
    slopes = sigmoid * (1.0 + hidden * (1.0 - sigmoid))
    feature_ids = col_index * col_width + jnp.arange(col_width, dtype=jnp.int32)
    target = (labels[:, None] == feature_ids[None, :]).astype(jnp.float32)
    out_grad = ((activated - target) * slopes).astype(jnp.bfloat16)
    grad_all = lax.all_gather(out_grad, "cols", axis=1, tiled=True)
    weight_terms = jnp.concatenate(
        [
            jnp.einsum("jnf,nc->jfc", first_all, out_grad, preferred_element_type=jnp.float32),
            jnp.einsum("jnf,nc->jfc", second_all, out_grad, preferred_element_type=jnp.float32),
        ],
        axis=1,
    ).reshape(col_devices * col_width, col_width)
    node_total = local_rows * row_devices
    weight_grad = row_all_reduce(weight_terms) / math.sqrt(node_total)
    agg_grad = jnp.einsum("nc,kc->nk", grad_all, w_rows, preferred_element_type=jnp.float32).astype(
        jnp.bfloat16
    )
    grad_rows = agg_grad.reshape(local_blocks, block_size, col_width)[tile_row]
    sent_terms = jnp.einsum(
        "tji,tjf->tif", tile_values, grad_rows, preferred_element_type=jnp.float32
    ).astype(jnp.bfloat16)
    slot_tile = (
        jnp.full((row_devices, capacity), tiles, jnp.int32)
        .at[owners, slot_rank]
        .set(jnp.arange(tiles, dtype=jnp.int32))
    )
    padded_terms = jnp.concatenate([sent_terms, jnp.zeros_like(sent_terms[:1])], axis=0)
    received = rows_exchange(padded_terms[slot_tile])
    placing = (wanted[:, :, None] == local_ids[None, None, :]).astype(jnp.float32)
    feature_grad = jnp.einsum(
        "scb,scif->bif", placing, received.astype(jnp.float32), precision=lax.Precision.HIGHEST
    ).reshape(local_rows, col_width)
    return (activated.astype(jnp.bfloat16), weight_grad, feature_grad.astype(jnp.bfloat16))


def solution(mesh):
    return jax.shard_map(
        per_device,
        mesh=mesh,
        in_specs=(
            P("rows", "cols"),
            P(),
            P("rows", None, None),
            P("rows"),
            P("rows", None),
            P("rows"),
            P("rows"),
        ),
        out_specs=(P("rows", "cols"), P(None, "cols"), P("rows", "cols")),
        check_vma=False,
    )
```

```python
import math

import jax
import jax.numpy as jnp
from jax import lax
from jax.sharding import PartitionSpec as P


def slot_ranks(owners):
    positions = jnp.arange(owners.shape[0], dtype=jnp.int32)
    earlier = (owners[:, None] == owners[None, :]) & (positions[None, :] < positions[:, None])
    return jnp.sum(earlier.astype(jnp.int32), axis=1)


def rows_exchange(x):
    return lax.all_to_all(x, "rows", split_axis=0, concat_axis=0, tiled=True)


def row_all_reduce(partial):
    row_devices = lax.axis_size("rows")
    k, c = partial.shape
    pieces = partial.reshape(row_devices, k // row_devices, c)
    reduced = jnp.sum(rows_exchange(pieces), axis=0)
    return lax.all_gather(reduced, "rows", axis=0, tiled=True)


def per_device(node_features, weight, tile_values, tile_row, source_owner, source_block, labels):
    local_rows, col_width = node_features.shape
    block_size = tile_values.shape[1]
    local_blocks = local_rows // block_size
    row_devices = lax.axis_size("rows")
    col_devices = lax.axis_size("cols")
    tiles = tile_values.shape[0]
    capacity = 2 * tiles // row_devices
    half = col_width // 2
    owners = source_owner[:, 0]
    slot_rank = slot_ranks(owners)
    local_ids = jnp.arange(local_blocks, dtype=jnp.int32)
    row_onehot = (tile_row[:, None] == local_ids[None, :]).astype(jnp.float32)
    tile_ids = jnp.arange(tiles, dtype=jnp.int32)
    in_slot = (owners[:, None, None] == jnp.arange(row_devices, dtype=jnp.int32)[None, :, None]) & (
        slot_rank[:, None, None] == jnp.arange(capacity, dtype=jnp.int32)[None, None, :]
    )
    request = jnp.sum(jnp.where(in_slot, source_block[:, None, None], 0), axis=0)
    slot_tile = jnp.sum(jnp.where(in_slot, tile_ids[:, None, None] - tiles, 0), axis=0) + tiles
    wanted = rows_exchange(request)
    own_blocks = node_features.reshape(local_blocks, block_size, col_width)
    outgoing = own_blocks[wanted]
    col_index = lax.axis_index("cols")
    w_columns = lax.dynamic_slice_in_dim(weight, col_index * col_width, col_width, 1)
    w_rows = lax.dynamic_slice_in_dim(weight, col_index * col_width, col_width, 0)
    w_split = w_columns.reshape(col_devices, col_width, col_width)

    def aggregate(part):
        source_rows = part[owners, slot_rank]
        products = jnp.einsum(
            "tij,tjf->tif", tile_values, source_rows, preferred_element_type=jnp.float32
        )
        summed = jnp.einsum("tb,tif->bif", row_onehot, products, precision=lax.Precision.HIGHEST)
        return summed.reshape(local_rows, part.shape[-1]).astype(jnp.bfloat16)

    first = aggregate(rows_exchange(outgoing[..., :half]))
    second_out, first = lax.optimization_barrier((outgoing[..., half:], first))
    first_all = lax.all_gather(first, "cols", axis=0, tiled=False)
    second = aggregate(rows_exchange(second_out))
    second_all = lax.all_gather(second, "cols", axis=0, tiled=False)
    hidden = jnp.einsum(
        "jnf,jfc->nc", first_all, w_split[:, :half], preferred_element_type=jnp.float32
    ) + jnp.einsum(
        "jnf,jfc->nc", second_all, w_split[:, half:], preferred_element_type=jnp.float32
    )
    sigmoid = jax.nn.sigmoid(hidden)
    activated = hidden * sigmoid
    slopes = sigmoid * (1.0 + hidden * (1.0 - sigmoid))
    feature_ids = col_index * col_width + jnp.arange(col_width, dtype=jnp.int32)
    target = (labels[:, None] == feature_ids[None, :]).astype(jnp.float32)
    out_grad = ((activated - target) * slopes).astype(jnp.bfloat16)
    grad_all = lax.all_gather(out_grad, "cols", axis=1, tiled=True)
    weight_terms = jnp.concatenate(
        [
            jnp.einsum("jnf,nc->jfc", first_all, out_grad, preferred_element_type=jnp.float32),
            jnp.einsum("jnf,nc->jfc", second_all, out_grad, preferred_element_type=jnp.float32),
        ],
        axis=1,
    ).reshape(col_devices * col_width, col_width)
    node_total = local_rows * row_devices
    weight_grad = row_all_reduce(weight_terms) / math.sqrt(node_total)
    agg_grad = jnp.einsum("nc,kc->nk", grad_all, w_rows, preferred_element_type=jnp.float32).astype(
        jnp.bfloat16
    )
    grad_rows = agg_grad.reshape(local_blocks, block_size, col_width)[tile_row]
    sent_terms = jnp.einsum(
        "tji,tjf->tif", tile_values, grad_rows, preferred_element_type=jnp.float32
    ).astype(jnp.bfloat16)
    padded_terms = jnp.concatenate([sent_terms, jnp.zeros_like(sent_terms[:1])], axis=0)
    received = rows_exchange(padded_terms[slot_tile])
    placing = (wanted[:, :, None] == local_ids[None, None, :]).astype(jnp.float32)
    feature_grad = jnp.einsum(
        "scb,scif->bif", placing, received.astype(jnp.float32), precision=lax.Precision.HIGHEST
    ).reshape(local_rows, col_width)
    return (activated.astype(jnp.bfloat16), weight_grad, feature_grad.astype(jnp.bfloat16))


def solution(mesh):
    return jax.shard_map(
        per_device,
        mesh=mesh,
        in_specs=(
            P("rows", "cols"),
            P(),
            P("rows", None, None),
            P("rows"),
            P("rows", None),
            P("rows"),
            P("rows"),
        ),
        out_specs=(P("rows", "cols"), P(None, "cols"), P("rows", "cols")),
        check_vma=False,
    )
```

```python
import math

import jax
import jax.numpy as jnp
from jax import lax
from jax.experimental import pallas as pl
from jax.experimental.pallas import tpu as pltpu
from jax.sharding import PartitionSpec as P

MESH = pl.DeviceIdType.MESH


def _index_exchange_kernel(x_ref, o_ref, send_sems, recv_sems):
    n = x_ref.shape[0]
    me = lax.axis_index("rows")
    barrier = pltpu.get_barrier_semaphore()

    def greet(k, carry):
        pl.semaphore_signal(
            barrier, 1, device_id={"rows": lax.rem(me + k, n)}, device_id_type=MESH
        )
        return carry

    lax.fori_loop(1, n, greet, 0)
    pl.semaphore_wait(barrier, n - 1)

    def outgoing(peer):
        return pltpu.make_async_remote_copy(
            src_ref=x_ref.at[peer], dst_ref=o_ref.at[me], send_sem=send_sems.at[peer],
            recv_sem=recv_sems.at[me], device_id={"rows": peer}, device_id_type=MESH)

    def incoming(src):
        return pltpu.make_async_remote_copy(
            src_ref=x_ref.at[src], dst_ref=o_ref.at[src], send_sem=send_sems.at[src],
            recv_sem=recv_sems.at[src], device_id={"rows": src}, device_id_type=MESH)

    def start(k, carry):
        outgoing(lax.rem(me + k, n)).start()
        return carry

    lax.fori_loop(1, n, start, 0)
    o_ref[me] = x_ref[me]

    def finish(k, carry):
        outgoing(lax.rem(me + k, n)).wait_send()
        incoming(lax.rem(me + n - k, n)).wait_recv()
        return carry

    lax.fori_loop(1, n, finish, 0)


def index_exchange(table):
    n, width = table.shape
    padded = jnp.zeros((n, 8, 128), jnp.int32).at[:, 0, :width].set(table)
    out = pl.pallas_call(
        _index_exchange_kernel,
        out_shape=jax.ShapeDtypeStruct(padded.shape, padded.dtype),
        in_specs=[pl.BlockSpec(memory_space=pltpu.VMEM)],
        out_specs=pl.BlockSpec(memory_space=pltpu.VMEM),
        scratch_shapes=[pltpu.SemaphoreType.DMA((n,)), pltpu.SemaphoreType.DMA((n,))],
        compiler_params=pltpu.CompilerParams(collective_id=0, has_side_effects=True),
    )(padded)
    return out[:, 0, :width]


def slot_ranks(owners):
    positions = jnp.arange(owners.shape[0], dtype=jnp.int32)
    earlier = (owners[:, None] == owners[None, :]) & (positions[None, :] < positions[:, None])
    return jnp.sum(earlier.astype(jnp.int32), axis=1)


def rows_exchange(x):
    return lax.all_to_all(x, "rows", split_axis=0, concat_axis=0, tiled=True)


def row_all_reduce(partial):
    row_devices = lax.axis_size("rows")
    k, c = partial.shape
    pieces = partial.reshape(row_devices, k // row_devices, c)
    reduced = jnp.sum(rows_exchange(pieces), axis=0)
    spread = jnp.broadcast_to(reduced[None], (row_devices,) + reduced.shape)
    return rows_exchange(spread).reshape(k, c)


def per_device(node_features, weight, tile_values, tile_row, source_owner, source_block, labels):
    local_rows, col_width = node_features.shape
    block_size = tile_values.shape[1]
    local_blocks = local_rows // block_size
    row_devices = lax.axis_size("rows")
    col_devices = lax.axis_size("cols")
    tiles = tile_values.shape[0]
    capacity = 2 * tiles // row_devices
    half = col_width // 2
    owners = source_owner[:, 0]
    slot_rank = slot_ranks(owners)
    local_ids = jnp.arange(local_blocks, dtype=jnp.int32)
    row_onehot = (tile_row[:, None] == local_ids[None, :]).astype(jnp.float32)
    tile_ids = jnp.arange(tiles, dtype=jnp.int32)
    in_slot = (owners[:, None, None] == jnp.arange(row_devices, dtype=jnp.int32)[None, :, None]) & (
        slot_rank[:, None, None] == jnp.arange(capacity, dtype=jnp.int32)[None, None, :]
    )
    request = jnp.sum(jnp.where(in_slot, source_block[:, None, None], 0), axis=0)
    slot_tile = jnp.sum(jnp.where(in_slot, tile_ids[:, None, None] - tiles, 0), axis=0) + tiles
    wanted = index_exchange(request)
    own_blocks = node_features.reshape(local_blocks, block_size, col_width)
    outgoing = own_blocks[wanted]
    col_index = lax.axis_index("cols")
    w_columns = lax.dynamic_slice_in_dim(weight, col_index * col_width, col_width, 1)
    w_rows = lax.dynamic_slice_in_dim(weight, col_index * col_width, col_width, 0)
    w_split = w_columns.reshape(col_devices, col_width, col_width)

    def aggregate(part):
        source_rows = part[owners, slot_rank]
        products = jnp.einsum(
            "tij,tjf->tif", tile_values, source_rows, preferred_element_type=jnp.float32
        )
        summed = jnp.einsum("tb,tif->bif", row_onehot, products, precision=lax.Precision.HIGHEST)
        return summed.reshape(local_rows, part.shape[-1]).astype(jnp.bfloat16)

    first = aggregate(rows_exchange(outgoing[..., :half]))
    second_out, first = lax.optimization_barrier((outgoing[..., half:], first))
    first_all = lax.all_gather(first, "cols", axis=0, tiled=False)
    second = aggregate(rows_exchange(second_out))
    second_all = lax.all_gather(second, "cols", axis=0, tiled=False)
    hidden = jnp.einsum(
        "jnf,jfc->nc", first_all, w_split[:, :half], preferred_element_type=jnp.float32
    ) + jnp.einsum(
        "jnf,jfc->nc", second_all, w_split[:, half:], preferred_element_type=jnp.float32
    )
    sigmoid = jax.nn.sigmoid(hidden)
    activated = hidden * sigmoid
    slopes = sigmoid * (1.0 + hidden * (1.0 - sigmoid))
    feature_ids = col_index * col_width + jnp.arange(col_width, dtype=jnp.int32)
    target = (labels[:, None] == feature_ids[None, :]).astype(jnp.float32)
    out_grad = ((activated - target) * slopes).astype(jnp.bfloat16)
    grad_all = lax.all_gather(out_grad, "cols", axis=1, tiled=True)
    weight_terms = jnp.concatenate(
        [
            jnp.einsum("jnf,nc->jfc", first_all, out_grad, preferred_element_type=jnp.float32),
            jnp.einsum("jnf,nc->jfc", second_all, out_grad, preferred_element_type=jnp.float32),
        ],
        axis=1,
    ).reshape(col_devices * col_width, col_width)
    node_total = local_rows * row_devices
    weight_grad = row_all_reduce(weight_terms) / math.sqrt(node_total)
    agg_grad = jnp.einsum("nc,kc->nk", grad_all, w_rows, preferred_element_type=jnp.float32).astype(
        jnp.bfloat16
    )
    grad_rows = agg_grad.reshape(local_blocks, block_size, col_width)[tile_row]
    sent_terms = jnp.einsum(
        "tji,tjf->tif", tile_values, grad_rows, preferred_element_type=jnp.float32
    ).astype(jnp.bfloat16)
    padded_terms = jnp.concatenate([sent_terms, jnp.zeros_like(sent_terms[:1])], axis=0)
    received = rows_exchange(padded_terms[slot_tile])
    placing = (wanted[:, :, None] == local_ids[None, None, :]).astype(jnp.float32)
    feature_grad = jnp.einsum(
        "scb,scif->bif", placing, received.astype(jnp.float32), precision=lax.Precision.HIGHEST
    ).reshape(local_rows, col_width)
    return (activated.astype(jnp.bfloat16), weight_grad, feature_grad.astype(jnp.bfloat16))


def solution(mesh):
    return jax.shard_map(
        per_device,
        mesh=mesh,
        in_specs=(
            P("rows", "cols"),
            P(),
            P("rows", None, None),
            P("rows"),
            P("rows", None),
            P("rows"),
            P("rows"),
        ),
        out_specs=(P("rows", "cols"), P(None, "cols"), P("rows", "cols")),
        check_vma=False,
    )
```

```python
import math

import jax
import jax.numpy as jnp
from jax import lax
from jax.experimental import pallas as pl
from jax.experimental.pallas import tpu as pltpu
from jax.sharding import PartitionSpec as P

MESH = pl.DeviceIdType.MESH


def _index_exchange_kernel(x_ref, o_ref, send_sems, recv_sems):
    n = x_ref.shape[0]
    me = lax.axis_index("rows")
    barrier = pltpu.get_barrier_semaphore()

    def greet(k, carry):
        pl.semaphore_signal(
            barrier, 1, device_id={"rows": lax.rem(me + k, n)}, device_id_type=MESH
        )
        return carry

    lax.fori_loop(1, n, greet, 0)
    pl.semaphore_wait(barrier, n - 1)

    def outgoing(peer):
        return pltpu.make_async_remote_copy(
            src_ref=x_ref.at[peer], dst_ref=o_ref.at[me], send_sem=send_sems.at[peer],
            recv_sem=recv_sems.at[me], device_id={"rows": peer}, device_id_type=MESH)

    def incoming(src):
        return pltpu.make_async_remote_copy(
            src_ref=x_ref.at[src], dst_ref=o_ref.at[src], send_sem=send_sems.at[src],
            recv_sem=recv_sems.at[src], device_id={"rows": src}, device_id_type=MESH)

    def start(k, carry):
        outgoing(lax.rem(me + k, n)).start()
        return carry

    lax.fori_loop(1, n, start, 0)
    o_ref[me] = x_ref[me]

    def finish(k, carry):
        outgoing(lax.rem(me + k, n)).wait_send()
        incoming(lax.rem(me + n - k, n)).wait_recv()
        return carry

    lax.fori_loop(1, n, finish, 0)


def index_exchange(table):
    n, width = table.shape
    padded = jnp.zeros((n, 8, 128), jnp.int32).at[:, 0, :width].set(table)
    out = pl.pallas_call(
        _index_exchange_kernel,
        out_shape=jax.ShapeDtypeStruct(padded.shape, padded.dtype),
        in_specs=[pl.BlockSpec(memory_space=pltpu.VMEM)],
        out_specs=pl.BlockSpec(memory_space=pltpu.VMEM),
        scratch_shapes=[pltpu.SemaphoreType.DMA((n,)), pltpu.SemaphoreType.DMA((n,))],
        compiler_params=pltpu.CompilerParams(collective_id=0, has_side_effects=True),
    )(padded)
    return out[:, 0, :width]


def _rows_gather_kernel(x_ref, o_ref, send_sems, recv_sems):
    n = o_ref.shape[0]
    me = lax.axis_index("rows")
    barrier = pltpu.get_barrier_semaphore()

    def greet(k, carry):
        pl.semaphore_signal(
            barrier, 1, device_id={"rows": lax.rem(me + k, n)}, device_id_type=MESH
        )
        return carry

    lax.fori_loop(1, n, greet, 0)
    pl.semaphore_wait(barrier, n - 1)

    def outgoing(peer):
        return pltpu.make_async_remote_copy(
            src_ref=x_ref, dst_ref=o_ref.at[me], send_sem=send_sems.at[peer],
            recv_sem=recv_sems.at[me], device_id={"rows": peer}, device_id_type=MESH)

    def incoming(src):
        return pltpu.make_async_remote_copy(
            src_ref=x_ref, dst_ref=o_ref.at[src], send_sem=send_sems.at[src],
            recv_sem=recv_sems.at[src], device_id={"rows": src}, device_id_type=MESH)

    def start(k, carry):
        outgoing(lax.rem(me + k, n)).start()
        return carry

    lax.fori_loop(1, n, start, 0)
    o_ref[me] = x_ref[...]

    def finish(k, carry):
        outgoing(lax.rem(me + k, n)).wait_send()
        incoming(lax.rem(me + n - k, n)).wait_recv()
        return carry

    lax.fori_loop(1, n, finish, 0)


def rows_gather(x):
    n = lax.axis_size("rows")
    return pl.pallas_call(
        _rows_gather_kernel,
        out_shape=jax.ShapeDtypeStruct((n,) + x.shape, x.dtype),
        in_specs=[pl.BlockSpec(memory_space=pltpu.VMEM)],
        out_specs=pl.BlockSpec(memory_space=pltpu.VMEM),
        scratch_shapes=[pltpu.SemaphoreType.DMA((n,)), pltpu.SemaphoreType.DMA((n,))],
        compiler_params=pltpu.CompilerParams(collective_id=1, has_side_effects=True),
        cost_estimate=pl.CostEstimate(
            flops=0, transcendentals=0, bytes_accessed=2 * n * x.size * x.dtype.itemsize
        ),
    )(x)


def slot_ranks(owners):
    positions = jnp.arange(owners.shape[0], dtype=jnp.int32)
    earlier = (owners[:, None] == owners[None, :]) & (positions[None, :] < positions[:, None])
    return jnp.sum(earlier.astype(jnp.int32), axis=1)


def rows_exchange(x):
    return lax.all_to_all(x, "rows", split_axis=0, concat_axis=0, tiled=True)


def row_all_reduce(partial):
    row_devices = lax.axis_size("rows")
    k, c = partial.shape
    pieces = partial.reshape(row_devices, k // row_devices, c)
    reduced = jnp.sum(rows_exchange(pieces), axis=0)
    return rows_gather(reduced).reshape(k, c)


def per_device(node_features, weight, tile_values, tile_row, source_owner, source_block, labels):
    local_rows, col_width = node_features.shape
    block_size = tile_values.shape[1]
    local_blocks = local_rows // block_size
    row_devices = lax.axis_size("rows")
    col_devices = lax.axis_size("cols")
    tiles = tile_values.shape[0]
    capacity = 2 * tiles // row_devices
    half = col_width // 2
    owners = source_owner[:, 0]
    slot_rank = slot_ranks(owners)
    local_ids = jnp.arange(local_blocks, dtype=jnp.int32)
    row_onehot = (tile_row[:, None] == local_ids[None, :]).astype(jnp.float32)
    tile_ids = jnp.arange(tiles, dtype=jnp.int32)
    in_slot = (owners[:, None, None] == jnp.arange(row_devices, dtype=jnp.int32)[None, :, None]) & (
        slot_rank[:, None, None] == jnp.arange(capacity, dtype=jnp.int32)[None, None, :]
    )
    request = jnp.sum(jnp.where(in_slot, source_block[:, None, None], 0), axis=0)
    slot_tile = jnp.sum(jnp.where(in_slot, tile_ids[:, None, None] - tiles, 0), axis=0) + tiles
    wanted = index_exchange(request)
    own_blocks = node_features.reshape(local_blocks, block_size, col_width)
    outgoing = own_blocks[wanted]
    col_index = lax.axis_index("cols")
    w_columns = lax.dynamic_slice_in_dim(weight, col_index * col_width, col_width, 1)
    w_rows = lax.dynamic_slice_in_dim(weight, col_index * col_width, col_width, 0)
    w_split = w_columns.reshape(col_devices, col_width, col_width)

    def aggregate(part):
        source_rows = part[owners, slot_rank]
        products = jnp.einsum(
            "tij,tjf->tif", tile_values, source_rows, preferred_element_type=jnp.float32
        )
        summed = jnp.einsum("tb,tif->bif", row_onehot, products, precision=lax.Precision.HIGHEST)
        return summed.reshape(local_rows, part.shape[-1]).astype(jnp.bfloat16)

    first = aggregate(rows_exchange(outgoing[..., :half]))
    second_out, first = lax.optimization_barrier((outgoing[..., half:], first))
    first_all = lax.all_gather(first, "cols", axis=0, tiled=False)
    second = aggregate(rows_exchange(second_out))
    second_all = lax.all_gather(second, "cols", axis=0, tiled=False)
    hidden = jnp.einsum(
        "jnf,jfc->nc", first_all, w_split[:, :half], preferred_element_type=jnp.float32
    ) + jnp.einsum(
        "jnf,jfc->nc", second_all, w_split[:, half:], preferred_element_type=jnp.float32
    )
    sigmoid = jax.nn.sigmoid(hidden)
    activated = hidden * sigmoid
    slopes = sigmoid * (1.0 + hidden * (1.0 - sigmoid))
    feature_ids = col_index * col_width + jnp.arange(col_width, dtype=jnp.int32)
    target = (labels[:, None] == feature_ids[None, :]).astype(jnp.float32)
    out_grad = ((activated - target) * slopes).astype(jnp.bfloat16)
    grad_all = lax.all_gather(out_grad, "cols", axis=1, tiled=True)
    weight_terms = jnp.concatenate(
        [
            jnp.einsum("jnf,nc->jfc", first_all, out_grad, preferred_element_type=jnp.float32),
            jnp.einsum("jnf,nc->jfc", second_all, out_grad, preferred_element_type=jnp.float32),
        ],
        axis=1,
    ).reshape(col_devices * col_width, col_width)
    node_total = local_rows * row_devices
    weight_grad = row_all_reduce(weight_terms) / math.sqrt(node_total)
    agg_grad = jnp.einsum("nc,kc->nk", grad_all, w_rows, preferred_element_type=jnp.float32).astype(
        jnp.bfloat16
    )
    grad_rows = agg_grad.reshape(local_blocks, block_size, col_width)[tile_row]
    sent_terms = jnp.einsum(
        "tji,tjf->tif", tile_values, grad_rows, preferred_element_type=jnp.float32
    ).astype(jnp.bfloat16)
    padded_terms = jnp.concatenate([sent_terms, jnp.zeros_like(sent_terms[:1])], axis=0)
    received = rows_exchange(padded_terms[slot_tile])
    placing = (wanted[:, :, None] == local_ids[None, None, :]).astype(jnp.float32)
    feature_grad = jnp.einsum(
        "scb,scif->bif", placing, received.astype(jnp.float32), precision=lax.Precision.HIGHEST
    ).reshape(local_rows, col_width)
    return (activated.astype(jnp.bfloat16), weight_grad, feature_grad.astype(jnp.bfloat16))


def solution(mesh):
    return jax.shard_map(
        per_device,
        mesh=mesh,
        in_specs=(
            P("rows", "cols"),
            P(),
            P("rows", None, None),
            P("rows"),
            P("rows", None),
            P("rows"),
            P("rows"),
        ),
        out_specs=(P("rows", "cols"), P(None, "cols"), P("rows", "cols")),
        check_vma=False,
    )
```

```python
import math

import jax
import jax.numpy as jnp
from jax import lax
from jax.sharding import PartitionSpec as P


def slot_ranks(owners):
    positions = jnp.arange(owners.shape[0], dtype=jnp.int32)
    earlier = (owners[:, None] == owners[None, :]) & (positions[None, :] < positions[:, None])
    return jnp.sum(earlier.astype(jnp.int32), axis=1)


def rows_exchange(x):
    return lax.all_to_all(x, "rows", split_axis=0, concat_axis=0, tiled=True)


def per_device(node_features, weight, tile_values, tile_row, source_owner, source_block, labels):
    local_rows, col_width = node_features.shape
    block_size = tile_values.shape[1]
    local_blocks = local_rows // block_size
    row_devices = lax.axis_size("rows")
    col_devices = lax.axis_size("cols")
    tiles = tile_values.shape[0]
    capacity = 2 * tiles // row_devices
    owners = source_owner[:, 0]
    slot_rank = slot_ranks(owners)
    local_ids = jnp.arange(local_blocks, dtype=jnp.int32)
    row_onehot = (tile_row[:, None] == local_ids[None, :]).astype(jnp.float32)
    tile_ids = jnp.arange(tiles, dtype=jnp.int32)
    in_slot = (owners[:, None, None] == jnp.arange(row_devices, dtype=jnp.int32)[None, :, None]) & (
        slot_rank[:, None, None] == jnp.arange(capacity, dtype=jnp.int32)[None, None, :]
    )
    request = jnp.sum(jnp.where(in_slot, source_block[:, None, None], 0), axis=0)
    slot_tile = jnp.sum(jnp.where(in_slot, tile_ids[:, None, None] - tiles, 0), axis=0) + tiles
    wanted = rows_exchange(request)
    own_blocks = node_features.reshape(local_blocks, block_size, col_width)
    incoming = rows_exchange(own_blocks[wanted])
    source_rows = incoming[owners, slot_rank]
    products = jnp.einsum(
        "tij,tjf->tif", tile_values, source_rows, preferred_element_type=jnp.float32
    )
    summed = jnp.einsum("tb,tif->bif", row_onehot, products, precision=lax.Precision.HIGHEST)
    aggregated = summed.reshape(local_rows, col_width).astype(jnp.bfloat16)
    aggregated_all = lax.all_gather(aggregated, "cols", axis=0, tiled=False)
    col_index = lax.axis_index("cols")
    w_columns = lax.dynamic_slice_in_dim(weight, col_index * col_width, col_width, 1)
    w_rows = lax.dynamic_slice_in_dim(weight, col_index * col_width, col_width, 0)
    w_split = w_columns.reshape(col_devices, col_width, col_width)
    hidden = jnp.einsum("jnf,jfc->nc", aggregated_all, w_split, preferred_element_type=jnp.float32)
    sigmoid = jax.nn.sigmoid(hidden)
    activated = hidden * sigmoid
    slopes = sigmoid * (1.0 + hidden * (1.0 - sigmoid))
    feature_ids = col_index * col_width + jnp.arange(col_width, dtype=jnp.int32)
    target = (labels[:, None] == feature_ids[None, :]).astype(jnp.float32)
    out_grad = ((activated - target) * slopes).astype(jnp.bfloat16)
    grad_all = lax.all_gather(out_grad, "cols", axis=1, tiled=True)
    weight_terms = jnp.einsum(
        "jnf,nc->jfc", aggregated_all, out_grad, preferred_element_type=jnp.float32
    ).reshape(col_devices * col_width, col_width)
    pieces = weight_terms.reshape(row_devices, -1, col_width)
    reduced = jnp.sum(rows_exchange(pieces), axis=0)
    high = reduced.astype(jnp.bfloat16)
    low = (reduced - high.astype(jnp.float32)).astype(jnp.bfloat16)
    chunk = jnp.concatenate([high, low], axis=0)
    chunk_rows = chunk.shape[0]
    agg_grad = jnp.einsum("nc,kc->nk", grad_all, w_rows, preferred_element_type=jnp.float32).astype(
        jnp.bfloat16
    )
    grad_rows = agg_grad.reshape(local_blocks, block_size, col_width)[tile_row]
    sent_terms = jnp.einsum(
        "tji,tjf->tif", tile_values, grad_rows, preferred_element_type=jnp.float32
    ).astype(jnp.bfloat16)
    padded_terms = jnp.concatenate([sent_terms, jnp.zeros_like(sent_terms[:1])], axis=0)
    send_terms = padded_terms[slot_tile].reshape(row_devices, capacity * block_size, col_width)
    payload = jnp.concatenate(
        [send_terms, jnp.broadcast_to(chunk[None], (row_devices,) + chunk.shape)], axis=1
    )
    arrived = rows_exchange(payload)
    received = arrived[:, : capacity * block_size].reshape(
        row_devices, capacity, block_size, col_width
    )
    half = chunk_rows // 2
    chunks = arrived[:, capacity * block_size :]
    total = chunks[:, :half].astype(jnp.float32) + chunks[:, half:].astype(jnp.float32)
    node_total = local_rows * row_devices
    weight_grad = total.reshape(col_devices * col_width, col_width) / math.sqrt(node_total)
    placing = (wanted[:, :, None] == local_ids[None, None, :]).astype(jnp.float32)
    feature_grad = jnp.einsum(
        "scb,scif->bif", placing, received.astype(jnp.float32), precision=lax.Precision.HIGHEST
    ).reshape(local_rows, col_width)
    return (activated.astype(jnp.bfloat16), weight_grad, feature_grad.astype(jnp.bfloat16))


def solution(mesh):
    return jax.shard_map(
        per_device,
        mesh=mesh,
        in_specs=(
            P("rows", "cols"),
            P(),
            P("rows", None, None),
            P("rows"),
            P("rows", None),
            P("rows"),
            P("rows"),
        ),
        out_specs=(P("rows", "cols"), P(None, "cols"), P("rows", "cols")),
        check_vma=False,
    )
```

```python
import math

import jax
import jax.numpy as jnp
from jax import lax
from jax.experimental import pallas as pl
from jax.experimental.pallas import tpu as pltpu
from jax.sharding import PartitionSpec as P

MESH = pl.DeviceIdType.MESH


def _cols_gather_kernel(x_ref, o_ref, send_sems, recv_sems):
    n = o_ref.shape[0]
    me = lax.axis_index("cols")
    barrier = pltpu.get_barrier_semaphore()
    for k in range(1, n):
        pl.semaphore_signal(
            barrier, 1, device_id={"cols": lax.rem(me + k, n)}, device_id_type=MESH
        )
    pl.semaphore_wait(barrier, n - 1)
    copies = []
    for k in range(1, n):
        peer = lax.rem(me + k, n)
        src = lax.rem(me + n - k, n)
        out = pltpu.make_async_remote_copy(
            src_ref=x_ref, dst_ref=o_ref.at[me], send_sem=send_sems.at[k],
            recv_sem=recv_sems.at[k], device_id={"cols": peer}, device_id_type=MESH)
        out.start()
        back = pltpu.make_async_remote_copy(
            src_ref=x_ref, dst_ref=o_ref.at[src], send_sem=send_sems.at[k],
            recv_sem=recv_sems.at[k], device_id={"cols": src}, device_id_type=MESH)
        copies.append((out, back))
    o_ref[me] = x_ref[...]
    for out, back in copies:
        out.wait_send()
        back.wait_recv()


def cols_gather(x):
    n = lax.axis_size("cols")
    return pl.pallas_call(
        _cols_gather_kernel,
        out_shape=jax.ShapeDtypeStruct((n,) + x.shape, x.dtype),
        in_specs=[pl.BlockSpec(memory_space=pltpu.VMEM)],
        out_specs=pl.BlockSpec(memory_space=pltpu.VMEM),
        scratch_shapes=[pltpu.SemaphoreType.DMA((n,)), pltpu.SemaphoreType.DMA((n,))],
        compiler_params=pltpu.CompilerParams(collective_id=2, has_side_effects=True),
    )(x)


def slot_ranks(owners):
    positions = jnp.arange(owners.shape[0], dtype=jnp.int32)
    earlier = (owners[:, None] == owners[None, :]) & (positions[None, :] < positions[:, None])
    return jnp.sum(earlier.astype(jnp.int32), axis=1)


def rows_exchange(x):
    return lax.all_to_all(x, "rows", split_axis=0, concat_axis=0, tiled=True)


def per_device(node_features, weight, tile_values, tile_row, source_owner, source_block, labels):
    local_rows, col_width = node_features.shape
    block_size = tile_values.shape[1]
    local_blocks = local_rows // block_size
    row_devices = lax.axis_size("rows")
    col_devices = lax.axis_size("cols")
    tiles = tile_values.shape[0]
    capacity = 2 * tiles // row_devices
    owners = source_owner[:, 0]
    slot_rank = slot_ranks(owners)
    local_ids = jnp.arange(local_blocks, dtype=jnp.int32)
    row_onehot = (tile_row[:, None] == local_ids[None, :]).astype(jnp.float32)
    tile_ids = jnp.arange(tiles, dtype=jnp.int32)
    in_slot = (owners[:, None, None] == jnp.arange(row_devices, dtype=jnp.int32)[None, :, None]) & (
        slot_rank[:, None, None] == jnp.arange(capacity, dtype=jnp.int32)[None, None, :]
    )
    request = jnp.sum(jnp.where(in_slot, source_block[:, None, None], 0), axis=0)
    slot_tile = jnp.sum(jnp.where(in_slot, tile_ids[:, None, None] - tiles, 0), axis=0) + tiles
    wanted = rows_exchange(request)
    own_blocks = node_features.reshape(local_blocks, block_size, col_width)
    incoming = rows_exchange(own_blocks[wanted])
    source_rows = incoming[owners, slot_rank]
    products = jnp.einsum(
        "tij,tjf->tif", tile_values, source_rows, preferred_element_type=jnp.float32
    )
    summed = jnp.einsum("tb,tif->bif", row_onehot, products, precision=lax.Precision.HIGHEST)
    aggregated = summed.reshape(local_rows, col_width).astype(jnp.bfloat16)
    packed = cols_gather(aggregated.reshape(local_rows // 2, 2 * col_width))
    aggregated_all = packed.reshape(col_devices, local_rows, col_width)
    col_index = lax.axis_index("cols")
    w_columns = lax.dynamic_slice_in_dim(weight, col_index * col_width, col_width, 1)
    w_rows = lax.dynamic_slice_in_dim(weight, col_index * col_width, col_width, 0)
    w_split = w_columns.reshape(col_devices, col_width, col_width)
    hidden = jnp.einsum("jnf,jfc->nc", aggregated_all, w_split, preferred_element_type=jnp.float32)
    sigmoid = jax.nn.sigmoid(hidden)
    activated = hidden * sigmoid
    slopes = sigmoid * (1.0 + hidden * (1.0 - sigmoid))
    feature_ids = col_index * col_width + jnp.arange(col_width, dtype=jnp.int32)
    target = (labels[:, None] == feature_ids[None, :]).astype(jnp.float32)
    out_grad = ((activated - target) * slopes).astype(jnp.bfloat16)
    grad_all = lax.all_gather(out_grad, "cols", axis=1, tiled=True)
    weight_terms = jnp.einsum(
        "jnf,nc->jfc", aggregated_all, out_grad, preferred_element_type=jnp.float32
    ).reshape(col_devices * col_width, col_width)
    pieces = weight_terms.reshape(row_devices, -1, col_width)
    reduced = jnp.sum(rows_exchange(pieces), axis=0)
    spread = jnp.broadcast_to(reduced[None], (row_devices,) + reduced.shape)
    node_total = local_rows * row_devices
    weight_grad = rows_exchange(spread).reshape(col_devices * col_width, col_width) / math.sqrt(
        node_total
    )
    agg_grad = jnp.einsum("nc,kc->nk", grad_all, w_rows, preferred_element_type=jnp.float32).astype(
        jnp.bfloat16
    )
    grad_rows = agg_grad.reshape(local_blocks, block_size, col_width)[tile_row]
    sent_terms = jnp.einsum(
        "tji,tjf->tif", tile_values, grad_rows, preferred_element_type=jnp.float32
    ).astype(jnp.bfloat16)
    padded_terms = jnp.concatenate([sent_terms, jnp.zeros_like(sent_terms[:1])], axis=0)
    received = rows_exchange(padded_terms[slot_tile])
    placing = (wanted[:, :, None] == local_ids[None, None, :]).astype(jnp.float32)
    feature_grad = jnp.einsum(
        "scb,scif->bif", placing, received.astype(jnp.float32), precision=lax.Precision.HIGHEST
    ).reshape(local_rows, col_width)
    return (activated.astype(jnp.bfloat16), weight_grad, feature_grad.astype(jnp.bfloat16))


def solution(mesh):
    return jax.shard_map(
        per_device,
        mesh=mesh,
        in_specs=(
            P("rows", "cols"),
            P(),
            P("rows", None, None),
            P("rows"),
            P("rows", None),
            P("rows"),
            P("rows"),
        ),
        out_specs=(P("rows", "cols"), P(None, "cols"), P("rows", "cols")),
        check_vma=False,
    )
```

```python
import math

import jax
import jax.numpy as jnp
from jax import lax
from jax.experimental import pallas as pl
from jax.experimental.pallas import tpu as pltpu
from jax.sharding import PartitionSpec as P

MESH = pl.DeviceIdType.MESH


def _cols_gather_kernel(x_ref, o_ref, send_sems, recv_sems):
    n = o_ref.shape[0]
    me = lax.axis_index("cols")
    barrier = pltpu.get_barrier_semaphore()
    for k in range(1, n):
        pl.semaphore_signal(
            barrier, 1, device_id={"cols": lax.rem(me + k, n)}, device_id_type=MESH
        )
    pl.semaphore_wait(barrier, n - 1)
    copies = []
    for k in range(1, n):
        peer = lax.rem(me + k, n)
        src = lax.rem(me + n - k, n)
        out = pltpu.make_async_remote_copy(
            src_ref=x_ref, dst_ref=o_ref.at[me], send_sem=send_sems.at[k],
            recv_sem=recv_sems.at[k], device_id={"cols": peer}, device_id_type=MESH)
        out.start()
        back = pltpu.make_async_remote_copy(
            src_ref=x_ref, dst_ref=o_ref.at[src], send_sem=send_sems.at[k],
            recv_sem=recv_sems.at[k], device_id={"cols": src}, device_id_type=MESH)
        copies.append((out, back))
    o_ref[me] = x_ref[...]
    for out, back in copies:
        out.wait_send()
        back.wait_recv()


def cols_gather(x):
    n = lax.axis_size("cols")
    return pl.pallas_call(
        _cols_gather_kernel,
        out_shape=jax.ShapeDtypeStruct((n,) + x.shape, x.dtype),
        in_specs=[pl.BlockSpec(memory_space=pltpu.VMEM)],
        out_specs=pl.BlockSpec(memory_space=pltpu.VMEM),
        scratch_shapes=[pltpu.SemaphoreType.DMA((n,)), pltpu.SemaphoreType.DMA((n,))],
        compiler_params=pltpu.CompilerParams(collective_id=2, has_side_effects=True),
    )(x)


def slot_ranks(owners):
    positions = jnp.arange(owners.shape[0], dtype=jnp.int32)
    earlier = (owners[:, None] == owners[None, :]) & (positions[None, :] < positions[:, None])
    return jnp.sum(earlier.astype(jnp.int32), axis=1)


def rows_exchange(x):
    return lax.all_to_all(x, "rows", split_axis=0, concat_axis=0, tiled=True)


def per_device(node_features, weight, tile_values, tile_row, source_owner, source_block, labels):
    local_rows, col_width = node_features.shape
    block_size = tile_values.shape[1]
    local_blocks = local_rows // block_size
    row_devices = lax.axis_size("rows")
    col_devices = lax.axis_size("cols")
    tiles = tile_values.shape[0]
    capacity = 2 * tiles // row_devices
    owners = source_owner[:, 0]
    slot_rank = slot_ranks(owners)
    local_ids = jnp.arange(local_blocks, dtype=jnp.int32)
    row_onehot = (tile_row[:, None] == local_ids[None, :]).astype(jnp.float32)
    tile_ids = jnp.arange(tiles, dtype=jnp.int32)
    in_slot = (owners[:, None, None] == jnp.arange(row_devices, dtype=jnp.int32)[None, :, None]) & (
        slot_rank[:, None, None] == jnp.arange(capacity, dtype=jnp.int32)[None, None, :]
    )
    request = jnp.sum(jnp.where(in_slot, source_block[:, None, None], 0), axis=0)
    slot_tile = jnp.sum(jnp.where(in_slot, tile_ids[:, None, None] - tiles, 0), axis=0) + tiles
    wanted = rows_exchange(request)
    own_blocks = node_features.reshape(local_blocks, block_size, col_width)
    incoming = rows_exchange(own_blocks[wanted])
    source_rows = incoming[owners, slot_rank]
    products = jnp.einsum(
        "tij,tjf->tif", tile_values, source_rows, preferred_element_type=jnp.float32
    )
    summed = jnp.einsum("tb,tif->bif", row_onehot, products, precision=lax.Precision.HIGHEST)
    aggregated = summed.reshape(local_rows, col_width).astype(jnp.bfloat16)
    aggregated_all = cols_gather(aggregated.T)
    col_index = lax.axis_index("cols")
    w_columns = lax.dynamic_slice_in_dim(weight, col_index * col_width, col_width, 1)
    w_rows = lax.dynamic_slice_in_dim(weight, col_index * col_width, col_width, 0)
    w_split = w_columns.reshape(col_devices, col_width, col_width)
    hidden = jnp.einsum("jfn,jfc->nc", aggregated_all, w_split, preferred_element_type=jnp.float32)
    sigmoid = jax.nn.sigmoid(hidden)
    activated = hidden * sigmoid
    slopes = sigmoid * (1.0 + hidden * (1.0 - sigmoid))
    feature_ids = col_index * col_width + jnp.arange(col_width, dtype=jnp.int32)
    target = (labels[:, None] == feature_ids[None, :]).astype(jnp.float32)
    out_grad = ((activated - target) * slopes).astype(jnp.bfloat16)
    grad_all = lax.all_gather(out_grad, "cols", axis=1, tiled=True)
    weight_terms = jnp.einsum(
        "jfn,nc->jfc", aggregated_all, out_grad, preferred_element_type=jnp.float32
    ).reshape(col_devices * col_width, col_width)
    pieces = weight_terms.reshape(row_devices, -1, col_width)
    reduced = jnp.sum(rows_exchange(pieces), axis=0)
    spread = jnp.broadcast_to(reduced[None], (row_devices,) + reduced.shape)
    node_total = local_rows * row_devices
    weight_grad = rows_exchange(spread).reshape(col_devices * col_width, col_width) / math.sqrt(
        node_total
    )
    agg_grad = jnp.einsum("nc,kc->nk", grad_all, w_rows, preferred_element_type=jnp.float32).astype(
        jnp.bfloat16
    )
    grad_rows = agg_grad.reshape(local_blocks, block_size, col_width)[tile_row]
    sent_terms = jnp.einsum(
        "tji,tjf->tfi", tile_values, grad_rows, preferred_element_type=jnp.float32
    ).astype(jnp.bfloat16)
    padded_terms = jnp.concatenate([sent_terms, jnp.zeros_like(sent_terms[:1])], axis=0)
    received = rows_exchange(padded_terms[slot_tile])
    placing = (wanted[:, :, None] == local_ids[None, None, :]).astype(jnp.float32)
    feature_grad = jnp.einsum(
        "scb,scfi->bif", placing, received.astype(jnp.float32), precision=lax.Precision.HIGHEST
    ).reshape(local_rows, col_width)
    return (activated.astype(jnp.bfloat16), weight_grad, feature_grad.astype(jnp.bfloat16))


def solution(mesh):
    return jax.shard_map(
        per_device,
        mesh=mesh,
        in_specs=(
            P("rows", "cols"),
            P(),
            P("rows", None, None),
            P("rows"),
            P("rows", None),
            P("rows"),
            P("rows"),
        ),
        out_specs=(P("rows", "cols"), P(None, "cols"), P("rows", "cols")),
        check_vma=False,
    )
```

```python
import math

import jax
import jax.numpy as jnp
from jax import lax
from jax.experimental import pallas as pl
from jax.experimental.pallas import tpu as pltpu
from jax.sharding import PartitionSpec as P

MESH = pl.DeviceIdType.MESH


def _cols_gather_kernel(x_ref, o_ref, send_sems, recv_sems):
    n = o_ref.shape[0]
    me = lax.axis_index("cols")
    barrier = pltpu.get_barrier_semaphore()
    for k in range(1, n):
        pl.semaphore_signal(
            barrier, 1, device_id={"cols": lax.rem(me + k, n)}, device_id_type=MESH
        )
    pl.semaphore_wait(barrier, n - 1)
    copies = []
    for k in range(1, n):
        peer = lax.rem(me + k, n)
        src = lax.rem(me + n - k, n)
        out = pltpu.make_async_remote_copy(
            src_ref=x_ref, dst_ref=o_ref.at[me], send_sem=send_sems.at[k],
            recv_sem=recv_sems.at[k], device_id={"cols": peer}, device_id_type=MESH)
        out.start()
        back = pltpu.make_async_remote_copy(
            src_ref=x_ref, dst_ref=o_ref.at[src], send_sem=send_sems.at[k],
            recv_sem=recv_sems.at[k], device_id={"cols": src}, device_id_type=MESH)
        copies.append((out, back))
    o_ref[me] = x_ref[...]
    for out, back in copies:
        out.wait_send()
        back.wait_recv()


def cols_gather(x):
    n = lax.axis_size("cols")
    return pl.pallas_call(
        _cols_gather_kernel,
        out_shape=jax.ShapeDtypeStruct((n,) + x.shape, x.dtype),
        in_specs=[pl.BlockSpec(memory_space=pltpu.VMEM)],
        out_specs=pl.BlockSpec(memory_space=pltpu.VMEM),
        scratch_shapes=[pltpu.SemaphoreType.DMA((n,)), pltpu.SemaphoreType.DMA((n,))],
        compiler_params=pltpu.CompilerParams(collective_id=2, has_side_effects=True),
    )(x)


def slot_ranks(owners):
    positions = jnp.arange(owners.shape[0], dtype=jnp.int32)
    earlier = (owners[:, None] == owners[None, :]) & (positions[None, :] < positions[:, None])
    return jnp.sum(earlier.astype(jnp.int32), axis=1)


def rows_exchange(x):
    return lax.all_to_all(x, "rows", split_axis=0, concat_axis=0, tiled=True)


def per_device(node_features, weight, tile_values, tile_row, source_owner, source_block, labels):
    local_rows, col_width = node_features.shape
    block_size = tile_values.shape[1]
    local_blocks = local_rows // block_size
    row_devices = lax.axis_size("rows")
    col_devices = lax.axis_size("cols")
    tiles = tile_values.shape[0]
    capacity = 2 * tiles // row_devices
    owners = source_owner[:, 0]
    slot_rank = slot_ranks(owners)
    local_ids = jnp.arange(local_blocks, dtype=jnp.int32)
    row_onehot = (tile_row[:, None] == local_ids[None, :]).astype(jnp.float32)
    in_slot = (owners[:, None, None] == jnp.arange(row_devices, dtype=jnp.int32)[None, :, None]) & (
        slot_rank[:, None, None] == jnp.arange(capacity, dtype=jnp.int32)[None, None, :]
    )
    request = jnp.sum(jnp.where(in_slot, source_block[:, None, None], 0), axis=0)
    wanted = rows_exchange(request)
    own_blocks = node_features.reshape(local_blocks, block_size, col_width)
    incoming = rows_exchange(own_blocks[wanted])
    source_rows = incoming[owners, slot_rank]
    products = jnp.einsum(
        "tij,tjf->tif", tile_values, source_rows, preferred_element_type=jnp.float32
    )
    summed = jnp.einsum("tb,tif->bif", row_onehot, products, precision=lax.Precision.HIGHEST)
    aggregated = summed.reshape(local_rows, col_width).astype(jnp.bfloat16)
    aggregated_all = cols_gather(aggregated.T)
    col_index = lax.axis_index("cols")
    w_columns = lax.dynamic_slice_in_dim(weight, col_index * col_width, col_width, 1)
    w_rows = lax.dynamic_slice_in_dim(weight, col_index * col_width, col_width, 0)
    w_split = w_columns.reshape(col_devices, col_width, col_width)
    hidden = jnp.einsum("jfn,jfc->nc", aggregated_all, w_split, preferred_element_type=jnp.float32)
    sigmoid = jax.nn.sigmoid(hidden)
    activated = hidden * sigmoid
    slopes = sigmoid * (1.0 + hidden * (1.0 - sigmoid))
    feature_ids = col_index * col_width + jnp.arange(col_width, dtype=jnp.int32)
    target = (labels[:, None] == feature_ids[None, :]).astype(jnp.float32)
    out_grad = ((activated - target) * slopes).astype(jnp.bfloat16)
    grad_all = lax.all_gather(out_grad, "cols", axis=1, tiled=True)
    weight_terms = jnp.einsum(
        "jfn,nc->jfc", aggregated_all, out_grad, preferred_element_type=jnp.float32
    ).reshape(col_devices * col_width, col_width)
    pieces = weight_terms.reshape(row_devices, -1, col_width)
    reduced = jnp.sum(rows_exchange(pieces), axis=0)
    spread = jnp.broadcast_to(reduced[None], (row_devices,) + reduced.shape)
    node_total = local_rows * row_devices
    weight_grad = rows_exchange(spread).reshape(col_devices * col_width, col_width) / math.sqrt(
        node_total
    )
    agg_grad = jnp.einsum("nc,kc->nk", grad_all, w_rows, preferred_element_type=jnp.float32).astype(
        jnp.bfloat16
    )
    grad_rows = agg_grad.reshape(local_blocks, block_size, col_width)[tile_row]
    sent_terms = jnp.einsum(
        "tji,tjf->tfi", tile_values, grad_rows, preferred_element_type=jnp.float32
    ).astype(jnp.bfloat16)
    slot_pick = in_slot.astype(jnp.bfloat16)
    send_terms = jnp.einsum(
        "tos,tfi->osfi", slot_pick, sent_terms, preferred_element_type=jnp.float32
    ).astype(jnp.bfloat16)
    received = rows_exchange(
        send_terms.reshape(row_devices, capacity * col_width, block_size)
    ).reshape(row_devices, capacity, col_width, block_size)
    placing = (wanted[:, :, None] == local_ids[None, None, :]).astype(jnp.bfloat16)
    feature_grad = jnp.einsum(
        "scb,scfi->bif", placing, received, preferred_element_type=jnp.float32
    ).reshape(local_rows, col_width)
    return (activated.astype(jnp.bfloat16), weight_grad, feature_grad.astype(jnp.bfloat16))


def solution(mesh):
    return jax.shard_map(
        per_device,
        mesh=mesh,
        in_specs=(
            P("rows", "cols"),
            P(),
            P("rows", None, None),
            P("rows"),
            P("rows", None),
            P("rows"),
            P("rows"),
        ),
        out_specs=(P("rows", "cols"), P(None, "cols"), P("rows", "cols")),
        check_vma=False,
    )
```

```python
import math

import jax
import jax.numpy as jnp
from jax import lax
from jax.experimental import pallas as pl
from jax.experimental.pallas import tpu as pltpu
from jax.sharding import PartitionSpec as P

MESH = pl.DeviceIdType.MESH


def _cols_gather_kernel(x_ref, o_ref, send_sems, recv_sems):
    n = o_ref.shape[0]
    me = lax.axis_index("cols")
    barrier = pltpu.get_barrier_semaphore()
    for k in range(1, n):
        pl.semaphore_signal(
            barrier, 1, device_id={"cols": lax.rem(me + k, n)}, device_id_type=MESH
        )
    pl.semaphore_wait(barrier, n - 1)
    copies = []
    for k in range(1, n):
        peer = lax.rem(me + k, n)
        src = lax.rem(me + n - k, n)
        out = pltpu.make_async_remote_copy(
            src_ref=x_ref, dst_ref=o_ref.at[me], send_sem=send_sems.at[k],
            recv_sem=recv_sems.at[k], device_id={"cols": peer}, device_id_type=MESH)
        out.start()
        back = pltpu.make_async_remote_copy(
            src_ref=x_ref, dst_ref=o_ref.at[src], send_sem=send_sems.at[k],
            recv_sem=recv_sems.at[k], device_id={"cols": src}, device_id_type=MESH)
        copies.append((out, back))
    o_ref[me] = x_ref[...]
    for out, back in copies:
        out.wait_send()
        back.wait_recv()


def cols_gather(x, collective_id):
    n = lax.axis_size("cols")
    return pl.pallas_call(
        _cols_gather_kernel,
        out_shape=jax.ShapeDtypeStruct((n,) + x.shape, x.dtype),
        in_specs=[pl.BlockSpec(memory_space=pltpu.VMEM)],
        out_specs=pl.BlockSpec(memory_space=pltpu.VMEM),
        scratch_shapes=[pltpu.SemaphoreType.DMA((n,)), pltpu.SemaphoreType.DMA((n,))],
        compiler_params=pltpu.CompilerParams(collective_id=collective_id, has_side_effects=True),
    )(x)


def slot_ranks(owners):
    positions = jnp.arange(owners.shape[0], dtype=jnp.int32)
    earlier = (owners[:, None] == owners[None, :]) & (positions[None, :] < positions[:, None])
    return jnp.sum(earlier.astype(jnp.int32), axis=1)


def rows_exchange(x):
    return lax.all_to_all(x, "rows", split_axis=0, concat_axis=0, tiled=True)


def per_device(node_features, weight, tile_values, tile_row, source_owner, source_block, labels):
    local_rows, col_width = node_features.shape
    block_size = tile_values.shape[1]
    local_blocks = local_rows // block_size
    row_devices = lax.axis_size("rows")
    col_devices = lax.axis_size("cols")
    tiles = tile_values.shape[0]
    capacity = 2 * tiles // row_devices
    owners = source_owner[:, 0]
    slot_rank = slot_ranks(owners)
    local_ids = jnp.arange(local_blocks, dtype=jnp.int32)
    row_onehot = (tile_row[:, None] == local_ids[None, :]).astype(jnp.float32)
    in_slot = (owners[:, None, None] == jnp.arange(row_devices, dtype=jnp.int32)[None, :, None]) & (
        slot_rank[:, None, None] == jnp.arange(capacity, dtype=jnp.int32)[None, None, :]
    )
    request = jnp.sum(jnp.where(in_slot, source_block[:, None, None], 0), axis=0)
    wanted = rows_exchange(request)
    own_blocks = node_features.reshape(local_blocks, block_size, col_width)
    incoming = rows_exchange(own_blocks[wanted])
    source_rows = incoming[owners, slot_rank]
    products = jnp.einsum(
        "tij,tjf->tif", tile_values, source_rows, preferred_element_type=jnp.float32
    )
    summed = jnp.einsum("tb,tif->bif", row_onehot, products, precision=lax.Precision.HIGHEST)
    aggregated = summed.reshape(local_rows, col_width).astype(jnp.bfloat16)
    aggregated_all = cols_gather(aggregated.T, 2)
    col_index = lax.axis_index("cols")
    w_columns = lax.dynamic_slice_in_dim(weight, col_index * col_width, col_width, 1)
    w_rows = lax.dynamic_slice_in_dim(weight, col_index * col_width, col_width, 0)
    w_split = w_columns.reshape(col_devices, col_width, col_width)
    hidden = jnp.einsum("jfn,jfc->nc", aggregated_all, w_split, preferred_element_type=jnp.float32)
    sigmoid = jax.nn.sigmoid(hidden)
    activated = hidden * sigmoid
    slopes = sigmoid * (1.0 + hidden * (1.0 - sigmoid))
    feature_ids = col_index * col_width + jnp.arange(col_width, dtype=jnp.int32)
    target = (labels[:, None] == feature_ids[None, :]).astype(jnp.float32)
    out_grad = ((activated - target) * slopes).astype(jnp.bfloat16)
    grad_all = cols_gather(out_grad.T, 3)
    weight_terms = jnp.einsum(
        "jfn,nc->jfc", aggregated_all, out_grad, preferred_element_type=jnp.float32
    ).reshape(col_devices * col_width, col_width)
    pieces = weight_terms.reshape(row_devices, -1, col_width)
    reduced = jnp.sum(rows_exchange(pieces), axis=0)
    spread = jnp.broadcast_to(reduced[None], (row_devices,) + reduced.shape)
    node_total = local_rows * row_devices
    weight_grad = rows_exchange(spread).reshape(col_devices * col_width, col_width) / math.sqrt(
        node_total
    )
    agg_grad = jnp.einsum(
        "jcn,kjc->nk",
        grad_all,
        w_rows.reshape(col_width, col_devices, col_width),
        preferred_element_type=jnp.float32,
    ).astype(jnp.bfloat16)
    grad_rows = agg_grad.reshape(local_blocks, block_size, col_width)[tile_row]
    sent_terms = jnp.einsum(
        "tji,tjf->tfi", tile_values, grad_rows, preferred_element_type=jnp.float32
    ).astype(jnp.bfloat16)
    slot_pick = in_slot.astype(jnp.bfloat16)
    send_terms = jnp.einsum(
        "tos,tfi->osfi", slot_pick, sent_terms, preferred_element_type=jnp.float32
    ).astype(jnp.bfloat16)
    received = rows_exchange(
        send_terms.reshape(row_devices, capacity * col_width, block_size)
    ).reshape(row_devices, capacity, col_width, block_size)
    placing = (wanted[:, :, None] == local_ids[None, None, :]).astype(jnp.bfloat16)
    feature_grad = jnp.einsum(
        "scb,scfi->bif", placing, received, preferred_element_type=jnp.float32
    ).reshape(local_rows, col_width)
    return (activated.astype(jnp.bfloat16), weight_grad, feature_grad.astype(jnp.bfloat16))


def solution(mesh):
    return jax.shard_map(
        per_device,
        mesh=mesh,
        in_specs=(
            P("rows", "cols"),
            P(),
            P("rows", None, None),
            P("rows"),
            P("rows", None),
            P("rows"),
            P("rows"),
        ),
        out_specs=(P("rows", "cols"), P(None, "cols"), P("rows", "cols")),
        check_vma=False,
    )
```

```python
import math

import jax
import jax.numpy as jnp
from jax import lax
from jax.experimental import pallas as pl
from jax.experimental.pallas import tpu as pltpu
from jax.sharding import PartitionSpec as P

MESH = pl.DeviceIdType.MESH


def _cols_gather_kernel(x_ref, o_ref, send_sems, recv_sems, pass_sems, take_sems):
    n = o_ref.shape[0]
    chips = n // 2
    me = lax.axis_index("cols")
    partner = me + 1 - 2 * lax.rem(me, 2)
    barrier = pltpu.get_barrier_semaphore()
    for k in range(1, chips):
        pl.semaphore_signal(
            barrier, 1, device_id={"cols": lax.rem(me + 2 * k, n)}, device_id_type=MESH
        )
    pl.semaphore_signal(barrier, 1, device_id={"cols": partner}, device_id_type=MESH)
    pl.semaphore_wait(barrier, chips)
    far = []
    for k in range(1, chips):
        out = pltpu.make_async_remote_copy(
            src_ref=x_ref, dst_ref=o_ref.at[me], send_sem=send_sems.at[k],
            recv_sem=recv_sems.at[k], device_id={"cols": lax.rem(me + 2 * k, n)},
            device_id_type=MESH)
        out.start()
        src = lax.rem(me + n - 2 * k, n)
        back = pltpu.make_async_remote_copy(
            src_ref=x_ref, dst_ref=o_ref.at[src], send_sem=send_sems.at[k],
            recv_sem=recv_sems.at[k], device_id={"cols": src}, device_id_type=MESH)
        far.append((out, back))
    near = [
        pltpu.make_async_remote_copy(
            src_ref=x_ref, dst_ref=o_ref.at[me], send_sem=pass_sems.at[0],
            recv_sem=take_sems.at[0], device_id={"cols": partner}, device_id_type=MESH)
    ]
    near[0].start()
    o_ref[me] = x_ref[...]
    for k in range(1, chips):
        out, back = far[k - 1]
        back.wait_recv()
        piece = lax.rem(me + n - 2 * k, n)
        hop = pltpu.make_async_remote_copy(
            src_ref=o_ref.at[piece], dst_ref=o_ref.at[piece], send_sem=pass_sems.at[k],
            recv_sem=take_sems.at[k], device_id={"cols": partner}, device_id_type=MESH)
        hop.start()
        near.append(hop)
    for k in range(chips):
        piece = lax.rem(partner + n - 2 * k, n)
        pltpu.make_async_remote_copy(
            src_ref=o_ref.at[piece], dst_ref=o_ref.at[piece], send_sem=pass_sems.at[k],
            recv_sem=take_sems.at[k], device_id={"cols": partner}, device_id_type=MESH
        ).wait_recv()
    for out, back in far:
        out.wait_send()
    for hop in near:
        hop.wait_send()


def cols_gather(x, collective_id):
    n = lax.axis_size("cols")
    return pl.pallas_call(
        _cols_gather_kernel,
        out_shape=jax.ShapeDtypeStruct((n,) + x.shape, x.dtype),
        in_specs=[pl.BlockSpec(memory_space=pltpu.VMEM)],
        out_specs=pl.BlockSpec(memory_space=pltpu.VMEM),
        scratch_shapes=[pltpu.SemaphoreType.DMA((n,))] * 4,
        compiler_params=pltpu.CompilerParams(collective_id=collective_id, has_side_effects=True),
    )(x)


def slot_ranks(owners):
    positions = jnp.arange(owners.shape[0], dtype=jnp.int32)
    earlier = (owners[:, None] == owners[None, :]) & (positions[None, :] < positions[:, None])
    return jnp.sum(earlier.astype(jnp.int32), axis=1)


def rows_exchange(x):
    return lax.all_to_all(x, "rows", split_axis=0, concat_axis=0, tiled=True)


def per_device(node_features, weight, tile_values, tile_row, source_owner, source_block, labels):
    local_rows, col_width = node_features.shape
    block_size = tile_values.shape[1]
    local_blocks = local_rows // block_size
    row_devices = lax.axis_size("rows")
    col_devices = lax.axis_size("cols")
    tiles = tile_values.shape[0]
    capacity = 2 * tiles // row_devices
    owners = source_owner[:, 0]
    slot_rank = slot_ranks(owners)
    local_ids = jnp.arange(local_blocks, dtype=jnp.int32)
    row_onehot = (tile_row[:, None] == local_ids[None, :]).astype(jnp.float32)
    in_slot = (owners[:, None, None] == jnp.arange(row_devices, dtype=jnp.int32)[None, :, None]) & (
        slot_rank[:, None, None] == jnp.arange(capacity, dtype=jnp.int32)[None, None, :]
    )
    request = jnp.sum(jnp.where(in_slot, source_block[:, None, None], 0), axis=0)
    wanted = rows_exchange(request)
    own_blocks = node_features.reshape(local_blocks, block_size, col_width)
    incoming = rows_exchange(own_blocks[wanted])
    source_rows = incoming[owners, slot_rank]
    products = jnp.einsum(
        "tij,tjf->tif", tile_values, source_rows, preferred_element_type=jnp.float32
    )
    summed = jnp.einsum("tb,tif->bif", row_onehot, products, precision=lax.Precision.HIGHEST)
    aggregated = summed.reshape(local_rows, col_width).astype(jnp.bfloat16)
    aggregated_all = cols_gather(aggregated.T, 2)
    col_index = lax.axis_index("cols")
    w_columns = lax.dynamic_slice_in_dim(weight, col_index * col_width, col_width, 1)
    w_rows = lax.dynamic_slice_in_dim(weight, col_index * col_width, col_width, 0)
    w_split = w_columns.reshape(col_devices, col_width, col_width)
    hidden = jnp.einsum("jfn,jfc->nc", aggregated_all, w_split, preferred_element_type=jnp.float32)
    sigmoid = jax.nn.sigmoid(hidden)
    activated = hidden * sigmoid
    slopes = sigmoid * (1.0 + hidden * (1.0 - sigmoid))
    feature_ids = col_index * col_width + jnp.arange(col_width, dtype=jnp.int32)
    target = (labels[:, None] == feature_ids[None, :]).astype(jnp.float32)
    out_grad = ((activated - target) * slopes).astype(jnp.bfloat16)
    grad_all = cols_gather(out_grad.T, 3)
    weight_terms = jnp.einsum(
        "jfn,nc->jfc", aggregated_all, out_grad, preferred_element_type=jnp.float32
    ).reshape(col_devices * col_width, col_width)
    pieces = weight_terms.reshape(row_devices, -1, col_width)
    reduced = jnp.sum(rows_exchange(pieces), axis=0)
    spread = jnp.broadcast_to(reduced[None], (row_devices,) + reduced.shape)
    node_total = local_rows * row_devices
    weight_grad = rows_exchange(spread).reshape(col_devices * col_width, col_width) / math.sqrt(
        node_total
    )
    agg_grad = jnp.einsum(
        "jcn,kjc->nk",
        grad_all,
        w_rows.reshape(col_width, col_devices, col_width),
        preferred_element_type=jnp.float32,
    ).astype(jnp.bfloat16)
    grad_rows = agg_grad.reshape(local_blocks, block_size, col_width)[tile_row]
    sent_terms = jnp.einsum(
        "tji,tjf->tfi", tile_values, grad_rows, preferred_element_type=jnp.float32
    ).astype(jnp.bfloat16)
    slot_pick = in_slot.astype(jnp.bfloat16)
    send_terms = jnp.einsum(
        "tos,tfi->osfi", slot_pick, sent_terms, preferred_element_type=jnp.float32
    ).astype(jnp.bfloat16)
    received = rows_exchange(
        send_terms.reshape(row_devices, capacity * col_width, block_size)
    ).reshape(row_devices, capacity, col_width, block_size)
    placing = (wanted[:, :, None] == local_ids[None, None, :]).astype(jnp.bfloat16)
    feature_grad = jnp.einsum(
        "scb,scfi->bif", placing, received, preferred_element_type=jnp.float32
    ).reshape(local_rows, col_width)
    return (activated.astype(jnp.bfloat16), weight_grad, feature_grad.astype(jnp.bfloat16))


def solution(mesh):
    return jax.shard_map(
        per_device,
        mesh=mesh,
        in_specs=(
            P("rows", "cols"),
            P(),
            P("rows", None, None),
            P("rows"),
            P("rows", None),
            P("rows"),
            P("rows"),
        ),
        out_specs=(P("rows", "cols"), P(None, "cols"), P("rows", "cols")),
        check_vma=False,
    )
```

```python
import math

import jax
import jax.numpy as jnp
from jax import lax
from jax.experimental import pallas as pl
from jax.experimental.pallas import tpu as pltpu
from jax.sharding import PartitionSpec as P

MESH = pl.DeviceIdType.MESH


def _cols_gather_kernel(x_ref, o_ref, send_sems, recv_sems, pass_sems, take_sems):
    n = o_ref.shape[0]
    chips = n // 2
    me = lax.axis_index("cols")
    partner = me + 1 - 2 * lax.rem(me, 2)
    barrier = pltpu.get_barrier_semaphore()
    for k in range(1, chips):
        pl.semaphore_signal(
            barrier, 1, device_id={"cols": lax.rem(me + 2 * k, n)}, device_id_type=MESH
        )
    pl.semaphore_signal(barrier, 1, device_id={"cols": partner}, device_id_type=MESH)
    pl.semaphore_wait(barrier, chips)
    far = []
    for k in range(1, chips):
        out = pltpu.make_async_remote_copy(
            src_ref=x_ref, dst_ref=o_ref.at[me], send_sem=send_sems.at[k],
            recv_sem=recv_sems.at[k], device_id={"cols": lax.rem(me + 2 * k, n)},
            device_id_type=MESH)
        out.start()
        src = lax.rem(me + n - 2 * k, n)
        back = pltpu.make_async_remote_copy(
            src_ref=x_ref, dst_ref=o_ref.at[src], send_sem=send_sems.at[k],
            recv_sem=recv_sems.at[k], device_id={"cols": src}, device_id_type=MESH)
        far.append((out, back))
    near = [
        pltpu.make_async_remote_copy(
            src_ref=x_ref, dst_ref=o_ref.at[me], send_sem=pass_sems.at[0],
            recv_sem=take_sems.at[0], device_id={"cols": partner}, device_id_type=MESH)
    ]
    near[0].start()
    o_ref[me] = x_ref[...]
    for k in range(1, chips):
        out, back = far[k - 1]
        back.wait_recv()
        piece = lax.rem(me + n - 2 * k, n)
        hop = pltpu.make_async_remote_copy(
            src_ref=o_ref.at[piece], dst_ref=o_ref.at[piece], send_sem=pass_sems.at[k],
            recv_sem=take_sems.at[k], device_id={"cols": partner}, device_id_type=MESH)
        hop.start()
        near.append(hop)
    for k in range(chips):
        piece = lax.rem(partner + n - 2 * k, n)
        pltpu.make_async_remote_copy(
            src_ref=o_ref.at[piece], dst_ref=o_ref.at[piece], send_sem=pass_sems.at[k],
            recv_sem=take_sems.at[k], device_id={"cols": partner}, device_id_type=MESH
        ).wait_recv()
    for out, back in far:
        out.wait_send()
    for hop in near:
        hop.wait_send()


def cols_gather(x, collective_id):
    n = lax.axis_size("cols")
    return pl.pallas_call(
        _cols_gather_kernel,
        out_shape=jax.ShapeDtypeStruct((n,) + x.shape, x.dtype),
        in_specs=[pl.BlockSpec(memory_space=pltpu.VMEM)],
        out_specs=pl.BlockSpec(memory_space=pltpu.VMEM),
        scratch_shapes=[pltpu.SemaphoreType.DMA((n,))] * 4,
        compiler_params=pltpu.CompilerParams(collective_id=collective_id, has_side_effects=True),
    )(x)


def slot_ranks(owners):
    positions = jnp.arange(owners.shape[0], dtype=jnp.int32)
    earlier = (owners[:, None] == owners[None, :]) & (positions[None, :] < positions[:, None])
    return jnp.sum(earlier.astype(jnp.int32), axis=1)


def rows_exchange(x):
    return lax.all_to_all(x, "rows", split_axis=0, concat_axis=0, tiled=True)


def per_device(node_features, weight, tile_values, tile_row, source_owner, source_block, labels):
    local_rows, col_width = node_features.shape
    block_size = tile_values.shape[1]
    local_blocks = local_rows // block_size
    row_devices = lax.axis_size("rows")
    col_devices = lax.axis_size("cols")
    tiles = tile_values.shape[0]
    capacity = 2 * tiles // row_devices
    owners = source_owner[:, 0]
    slot_rank = slot_ranks(owners)
    local_ids = jnp.arange(local_blocks, dtype=jnp.int32)
    row_onehot = (tile_row[:, None] == local_ids[None, :]).astype(jnp.float32)
    in_slot = (owners[:, None, None] == jnp.arange(row_devices, dtype=jnp.int32)[None, :, None]) & (
        slot_rank[:, None, None] == jnp.arange(capacity, dtype=jnp.int32)[None, None, :]
    )
    request = jnp.sum(jnp.where(in_slot, source_block[:, None, None], 0), axis=0)
    wanted = rows_exchange(request)
    own_blocks = node_features.reshape(local_blocks, block_size, col_width)
    incoming = rows_exchange(own_blocks[wanted])
    source_rows = incoming[owners, slot_rank]
    products = jnp.einsum(
        "tij,tjf->tif", tile_values, source_rows, preferred_element_type=jnp.float32
    )
    summed = jnp.einsum("tb,tif->bif", row_onehot, products, precision=lax.Precision.HIGHEST)
    aggregated = summed.reshape(local_rows, col_width).astype(jnp.bfloat16)
    aggregated_all = cols_gather(aggregated.T, 2)
    col_index = lax.axis_index("cols")
    w_columns = lax.dynamic_slice_in_dim(weight, col_index * col_width, col_width, 1)
    w_rows = lax.dynamic_slice_in_dim(weight, col_index * col_width, col_width, 0)
    w_split = w_columns.reshape(col_devices, col_width, col_width)
    hidden = jnp.einsum("jfn,jfc->nc", aggregated_all, w_split, preferred_element_type=jnp.float32)
    sigmoid = jax.nn.sigmoid(hidden)
    activated = hidden * sigmoid
    slopes = sigmoid * (1.0 + hidden * (1.0 - sigmoid))
    feature_ids = col_index * col_width + jnp.arange(col_width, dtype=jnp.int32)
    target = (labels[:, None] == feature_ids[None, :]).astype(jnp.float32)
    out_grad = ((activated - target) * slopes).astype(jnp.bfloat16)
    grad_all = cols_gather(out_grad.T, 3)
    weight_terms = jnp.einsum(
        "jfn,nc->jfc", aggregated_all, out_grad, preferred_element_type=jnp.float32
    ).reshape(col_devices * col_width, col_width)
    pieces = weight_terms.reshape(row_devices, -1, col_width)
    reduced = jnp.sum(rows_exchange(pieces), axis=0)
    agg_grad = jnp.einsum(
        "jcn,kjc->nk",
        grad_all,
        w_rows.reshape(col_width, col_devices, col_width),
        preferred_element_type=jnp.float32,
    ).astype(jnp.bfloat16)
    grad_rows = agg_grad.reshape(local_blocks, block_size, col_width)[tile_row]
    sent_terms = jnp.einsum(
        "tji,tjf->tfi", tile_values, grad_rows, preferred_element_type=jnp.float32
    ).astype(jnp.bfloat16)
    slot_pick = in_slot.astype(jnp.bfloat16)
    send_terms = jnp.einsum(
        "tos,tfi->osfi", slot_pick, sent_terms, preferred_element_type=jnp.float32
    ).astype(jnp.bfloat16)
    received = rows_exchange(
        send_terms.reshape(row_devices, capacity * col_width, block_size)
    ).reshape(row_devices, capacity, col_width, block_size)
    reduced, received = lax.optimization_barrier((reduced, received))
    spread = jnp.broadcast_to(reduced[None], (row_devices,) + reduced.shape)
    node_total = local_rows * row_devices
    weight_grad = rows_exchange(spread).reshape(col_devices * col_width, col_width) / math.sqrt(
        node_total
    )
    placing = (wanted[:, :, None] == local_ids[None, None, :]).astype(jnp.bfloat16)
    feature_grad = jnp.einsum(
        "scb,scfi->bif", placing, received, preferred_element_type=jnp.float32
    ).reshape(local_rows, col_width)
    return (activated.astype(jnp.bfloat16), weight_grad, feature_grad.astype(jnp.bfloat16))


def solution(mesh):
    return jax.shard_map(
        per_device,
        mesh=mesh,
        in_specs=(
            P("rows", "cols"),
            P(),
            P("rows", None, None),
            P("rows"),
            P("rows", None),
            P("rows"),
            P("rows"),
        ),
        out_specs=(P("rows", "cols"), P(None, "cols"), P("rows", "cols")),
        check_vma=False,
    )
```

```python
import math

import jax
import jax.numpy as jnp
from jax import lax
from jax.experimental import pallas as pl
from jax.experimental.pallas import tpu as pltpu
from jax.sharding import PartitionSpec as P

MESH = pl.DeviceIdType.MESH


def _cols_gather_kernel(x_ref, o_ref, send_sems, recv_sems, pass_sems, take_sems):
    n = o_ref.shape[0]
    chips = n // 2
    me = lax.axis_index("cols")
    partner = me + 1 - 2 * lax.rem(me, 2)
    barrier = pltpu.get_barrier_semaphore()
    for k in range(1, chips):
        pl.semaphore_signal(
            barrier, 1, device_id={"cols": lax.rem(me + 2 * k, n)}, device_id_type=MESH
        )
    pl.semaphore_signal(barrier, 1, device_id={"cols": partner}, device_id_type=MESH)
    pl.semaphore_wait(barrier, chips)
    far = []
    for k in range(1, chips):
        out = pltpu.make_async_remote_copy(
            src_ref=x_ref, dst_ref=o_ref.at[me], send_sem=send_sems.at[k],
            recv_sem=recv_sems.at[k], device_id={"cols": lax.rem(me + 2 * k, n)},
            device_id_type=MESH)
        out.start()
        src = lax.rem(me + n - 2 * k, n)
        back = pltpu.make_async_remote_copy(
            src_ref=x_ref, dst_ref=o_ref.at[src], send_sem=send_sems.at[k],
            recv_sem=recv_sems.at[k], device_id={"cols": src}, device_id_type=MESH)
        far.append((out, back))
    near = [
        pltpu.make_async_remote_copy(
            src_ref=x_ref, dst_ref=o_ref.at[me], send_sem=pass_sems.at[0],
            recv_sem=take_sems.at[0], device_id={"cols": partner}, device_id_type=MESH)
    ]
    near[0].start()
    o_ref[me] = x_ref[...]
    for k in range(1, chips):
        out, back = far[k - 1]
        back.wait_recv()
        piece = lax.rem(me + n - 2 * k, n)
        hop = pltpu.make_async_remote_copy(
            src_ref=o_ref.at[piece], dst_ref=o_ref.at[piece], send_sem=pass_sems.at[k],
            recv_sem=take_sems.at[k], device_id={"cols": partner}, device_id_type=MESH)
        hop.start()
        near.append(hop)
    for k in range(chips):
        piece = lax.rem(partner + n - 2 * k, n)
        pltpu.make_async_remote_copy(
            src_ref=o_ref.at[piece], dst_ref=o_ref.at[piece], send_sem=pass_sems.at[k],
            recv_sem=take_sems.at[k], device_id={"cols": partner}, device_id_type=MESH
        ).wait_recv()
    for out, back in far:
        out.wait_send()
    for hop in near:
        hop.wait_send()


def cols_gather(x, collective_id):
    n = lax.axis_size("cols")
    return pl.pallas_call(
        _cols_gather_kernel,
        out_shape=jax.ShapeDtypeStruct((n,) + x.shape, x.dtype),
        in_specs=[pl.BlockSpec(memory_space=pltpu.VMEM)],
        out_specs=pl.BlockSpec(memory_space=pltpu.VMEM),
        scratch_shapes=[pltpu.SemaphoreType.DMA((n,))] * 4,
        compiler_params=pltpu.CompilerParams(collective_id=collective_id, has_side_effects=True),
    )(x)


def slot_ranks(owners):
    positions = jnp.arange(owners.shape[0], dtype=jnp.int32)
    earlier = (owners[:, None] == owners[None, :]) & (positions[None, :] < positions[:, None])
    return jnp.sum(earlier.astype(jnp.int32), axis=1)


def rows_exchange(x):
    return lax.all_to_all(x, "rows", split_axis=0, concat_axis=0, tiled=True)


def per_device(node_features, weight, tile_values, tile_row, source_owner, source_block, labels):
    local_rows, col_width = node_features.shape
    block_size = tile_values.shape[1]
    local_blocks = local_rows // block_size
    row_devices = lax.axis_size("rows")
    col_devices = lax.axis_size("cols")
    tiles = tile_values.shape[0]
    capacity = 2 * tiles // row_devices
    owners = source_owner[:, 0]
    slot_rank = slot_ranks(owners)
    local_ids = jnp.arange(local_blocks, dtype=jnp.int32)
    row_onehot = (tile_row[:, None] == local_ids[None, :]).astype(jnp.float32)
    in_slot = (owners[:, None, None] == jnp.arange(row_devices, dtype=jnp.int32)[None, :, None]) & (
        slot_rank[:, None, None] == jnp.arange(capacity, dtype=jnp.int32)[None, None, :]
    )
    request = jnp.sum(jnp.where(in_slot, source_block[:, None, None], 0), axis=0)
    wanted = rows_exchange(request)
    own_blocks = node_features.reshape(local_blocks, block_size, col_width)
    wanted_pick = (wanted[:, :, None] == local_ids[None, None, :]).astype(jnp.bfloat16)
    outgoing = jnp.einsum(
        "osb,bif->osif", wanted_pick, own_blocks, preferred_element_type=jnp.float32
    ).astype(jnp.bfloat16)
    incoming = rows_exchange(outgoing)
    source_rows = jnp.einsum(
        "tos,osif->tif", in_slot.astype(jnp.bfloat16), incoming, preferred_element_type=jnp.float32
    ).astype(jnp.bfloat16)
    products = jnp.einsum(
        "tij,tjf->tif", tile_values, source_rows, preferred_element_type=jnp.float32
    )
    summed = jnp.einsum("tb,tif->bif", row_onehot, products, precision=lax.Precision.HIGHEST)
    aggregated = summed.reshape(local_rows, col_width).astype(jnp.bfloat16)
    aggregated_all = cols_gather(aggregated.T, 2)
    col_index = lax.axis_index("cols")
    w_columns = lax.dynamic_slice_in_dim(weight, col_index * col_width, col_width, 1)
    w_rows = lax.dynamic_slice_in_dim(weight, col_index * col_width, col_width, 0)
    w_split = w_columns.reshape(col_devices, col_width, col_width)
    hidden = jnp.einsum("jfn,jfc->nc", aggregated_all, w_split, preferred_element_type=jnp.float32)
    sigmoid = jax.nn.sigmoid(hidden)
    activated = hidden * sigmoid
    slopes = sigmoid * (1.0 + hidden * (1.0 - sigmoid))
    feature_ids = col_index * col_width + jnp.arange(col_width, dtype=jnp.int32)
    target = (labels[:, None] == feature_ids[None, :]).astype(jnp.float32)
    out_grad = ((activated - target) * slopes).astype(jnp.bfloat16)
    grad_all = cols_gather(out_grad.T, 3)
    weight_terms = jnp.einsum(
        "jfn,nc->jfc", aggregated_all, out_grad, preferred_element_type=jnp.float32
    ).reshape(col_devices * col_width, col_width)
    pieces = weight_terms.reshape(row_devices, -1, col_width)
    reduced = jnp.sum(rows_exchange(pieces), axis=0)
    spread = jnp.broadcast_to(reduced[None], (row_devices,) + reduced.shape)
    node_total = local_rows * row_devices
    weight_grad = rows_exchange(spread).reshape(col_devices * col_width, col_width) / math.sqrt(
        node_total
    )
    agg_grad = jnp.einsum(
        "jcn,kjc->nk",
        grad_all,
        w_rows.reshape(col_width, col_devices, col_width),
        preferred_element_type=jnp.float32,
    ).astype(jnp.bfloat16)
    grad_rows = agg_grad.reshape(local_blocks, block_size, col_width)[tile_row]
    sent_terms = jnp.einsum(
        "tji,tjf->tfi", tile_values, grad_rows, preferred_element_type=jnp.float32
    ).astype(jnp.bfloat16)
    slot_pick = in_slot.astype(jnp.bfloat16)
    send_terms = jnp.einsum(
        "tos,tfi->osfi", slot_pick, sent_terms, preferred_element_type=jnp.float32
    ).astype(jnp.bfloat16)
    received = rows_exchange(
        send_terms.reshape(row_devices, capacity * col_width, block_size)
    ).reshape(row_devices, capacity, col_width, block_size)
    placing = (wanted[:, :, None] == local_ids[None, None, :]).astype(jnp.bfloat16)
    feature_grad = jnp.einsum(
        "scb,scfi->bif", placing, received, preferred_element_type=jnp.float32
    ).reshape(local_rows, col_width)
    return (activated.astype(jnp.bfloat16), weight_grad, feature_grad.astype(jnp.bfloat16))


def solution(mesh):
    return jax.shard_map(
        per_device,
        mesh=mesh,
        in_specs=(
            P("rows", "cols"),
            P(),
            P("rows", None, None),
            P("rows"),
            P("rows", None),
            P("rows"),
            P("rows"),
        ),
        out_specs=(P("rows", "cols"), P(None, "cols"), P("rows", "cols")),
        check_vma=False,
    )
```

```python
import math

import jax
import jax.numpy as jnp
from jax import lax
from jax.experimental import pallas as pl
from jax.experimental.pallas import tpu as pltpu
from jax.sharding import PartitionSpec as P

MESH = pl.DeviceIdType.MESH


def _cols_gather_kernel(x_ref, o_ref, send_sems, recv_sems, pass_sems, take_sems):
    n = o_ref.shape[0]
    chips = n // 2
    me = lax.axis_index("cols")
    partner = me + 1 - 2 * lax.rem(me, 2)
    barrier = pltpu.get_barrier_semaphore()
    for k in range(1, chips):
        pl.semaphore_signal(
            barrier, 1, device_id={"cols": lax.rem(me + 2 * k, n)}, device_id_type=MESH
        )
    pl.semaphore_signal(barrier, 1, device_id={"cols": partner}, device_id_type=MESH)
    pl.semaphore_wait(barrier, chips)
    far = []
    for k in range(1, chips):
        out = pltpu.make_async_remote_copy(
            src_ref=x_ref, dst_ref=o_ref.at[me], send_sem=send_sems.at[k],
            recv_sem=recv_sems.at[k], device_id={"cols": lax.rem(me + 2 * k, n)},
            device_id_type=MESH)
        out.start()
        src = lax.rem(me + n - 2 * k, n)
        back = pltpu.make_async_remote_copy(
            src_ref=x_ref, dst_ref=o_ref.at[src], send_sem=send_sems.at[k],
            recv_sem=recv_sems.at[k], device_id={"cols": src}, device_id_type=MESH)
        far.append((out, back))
    near = [
        pltpu.make_async_remote_copy(
            src_ref=x_ref, dst_ref=o_ref.at[me], send_sem=pass_sems.at[0],
            recv_sem=take_sems.at[0], device_id={"cols": partner}, device_id_type=MESH)
    ]
    near[0].start()
    o_ref[me] = x_ref[...]
    for k in range(1, chips):
        out, back = far[k - 1]
        back.wait_recv()
        piece = lax.rem(me + n - 2 * k, n)
        hop = pltpu.make_async_remote_copy(
            src_ref=o_ref.at[piece], dst_ref=o_ref.at[piece], send_sem=pass_sems.at[k],
            recv_sem=take_sems.at[k], device_id={"cols": partner}, device_id_type=MESH)
        hop.start()
        near.append(hop)
    for k in range(chips):
        piece = lax.rem(partner + n - 2 * k, n)
        pltpu.make_async_remote_copy(
            src_ref=o_ref.at[piece], dst_ref=o_ref.at[piece], send_sem=pass_sems.at[k],
            recv_sem=take_sems.at[k], device_id={"cols": partner}, device_id_type=MESH
        ).wait_recv()
    for out, back in far:
        out.wait_send()
    for hop in near:
        hop.wait_send()


def cols_gather(x, collective_id):
    n = lax.axis_size("cols")
    return pl.pallas_call(
        _cols_gather_kernel,
        out_shape=jax.ShapeDtypeStruct((n,) + x.shape, x.dtype),
        in_specs=[pl.BlockSpec(memory_space=pltpu.VMEM)],
        out_specs=pl.BlockSpec(memory_space=pltpu.VMEM),
        scratch_shapes=[pltpu.SemaphoreType.DMA((n,))] * 4,
        compiler_params=pltpu.CompilerParams(collective_id=collective_id, has_side_effects=True),
    )(x)


def slot_ranks(owners):
    positions = jnp.arange(owners.shape[0], dtype=jnp.int32)
    earlier = (owners[:, None] == owners[None, :]) & (positions[None, :] < positions[:, None])
    return jnp.sum(earlier.astype(jnp.int32), axis=1)


def rows_exchange(x):
    return lax.all_to_all(x, "rows", split_axis=0, concat_axis=0, tiled=True)


def per_device(node_features, weight, tile_values, tile_row, source_owner, source_block, labels):
    local_rows, col_width = node_features.shape
    block_size = tile_values.shape[1]
    local_blocks = local_rows // block_size
    row_devices = lax.axis_size("rows")
    col_devices = lax.axis_size("cols")
    tiles = tile_values.shape[0]
    capacity = 2 * tiles // row_devices
    owners = source_owner[:, 0]
    slot_rank = slot_ranks(owners)
    local_ids = jnp.arange(local_blocks, dtype=jnp.int32)
    row_onehot = (tile_row[:, None] == local_ids[None, :]).astype(jnp.float32)
    in_slot = (owners[:, None, None] == jnp.arange(row_devices, dtype=jnp.int32)[None, :, None]) & (
        slot_rank[:, None, None] == jnp.arange(capacity, dtype=jnp.int32)[None, None, :]
    )
    request = jnp.sum(jnp.where(in_slot, source_block[:, None, None], 0), axis=0)
    wanted = rows_exchange(request)
    own_blocks = node_features.reshape(local_blocks, block_size, col_width)
    incoming = rows_exchange(own_blocks[wanted])
    source_rows = incoming[owners, slot_rank]
    products = jnp.einsum(
        "tij,tjf->tif", tile_values, source_rows, preferred_element_type=jnp.float32
    )
    summed = jnp.einsum("tb,tif->bif", row_onehot, products, precision=lax.Precision.HIGHEST)
    aggregated = summed.reshape(local_rows, col_width).astype(jnp.bfloat16)
    aggregated_all = cols_gather(aggregated.T, 2)
    col_index = lax.axis_index("cols")
    w_columns = lax.dynamic_slice_in_dim(weight, col_index * col_width, col_width, 1)
    w_rows = lax.dynamic_slice_in_dim(weight, col_index * col_width, col_width, 0)
    w_split = w_columns.reshape(col_devices, col_width, col_width)
    hidden = jnp.einsum("jfn,jfc->nc", aggregated_all, w_split, preferred_element_type=jnp.float32)
    sigmoid = jax.nn.sigmoid(hidden)
    activated = hidden * sigmoid
    slopes = sigmoid * (1.0 + hidden * (1.0 - sigmoid))
    feature_ids = col_index * col_width + jnp.arange(col_width, dtype=jnp.int32)
    target = (labels[:, None] == feature_ids[None, :]).astype(jnp.float32)
    out_grad = ((activated - target) * slopes).astype(jnp.bfloat16)
    grad_all = cols_gather(out_grad.T, 3)
    weight_terms = jnp.einsum(
        "jfn,nc->jfc", aggregated_all, out_grad, preferred_element_type=jnp.float32
    ).reshape(col_devices * col_width, col_width)
    pieces = weight_terms.reshape(row_devices, -1, col_width)
    reduced = jnp.sum(rows_exchange(pieces), axis=0)
    high = reduced.astype(jnp.bfloat16)
    low = (reduced - high.astype(jnp.float32)).astype(jnp.bfloat16)
    chunk = jnp.concatenate([high, low], axis=0).reshape(-1, block_size)
    agg_grad = jnp.einsum(
        "jcn,kjc->nk",
        grad_all,
        w_rows.reshape(col_width, col_devices, col_width),
        preferred_element_type=jnp.float32,
    ).astype(jnp.bfloat16)
    grad_rows = agg_grad.reshape(local_blocks, block_size, col_width)[tile_row]
    sent_terms = jnp.einsum(
        "tji,tjf->tfi", tile_values, grad_rows, preferred_element_type=jnp.float32
    ).astype(jnp.bfloat16)
    slot_pick = in_slot.astype(jnp.bfloat16)
    send_terms = jnp.einsum(
        "tos,tfi->osfi", slot_pick, sent_terms, preferred_element_type=jnp.float32
    ).astype(jnp.bfloat16)
    payload = jnp.concatenate(
        [
            send_terms.reshape(row_devices, capacity * col_width, block_size),
            jnp.broadcast_to(chunk[None], (row_devices,) + chunk.shape),
        ],
        axis=1,
    )
    arrived = rows_exchange(payload)
    received = arrived[:, : capacity * col_width].reshape(
        row_devices, capacity, col_width, block_size
    )
    parts = arrived[:, capacity * col_width :].reshape(row_devices, 2, -1, col_width)
    node_total = local_rows * row_devices
    weight_grad = (parts[:, 0].astype(jnp.float32) + parts[:, 1].astype(jnp.float32)).reshape(
        col_devices * col_width, col_width
    ) / math.sqrt(node_total)
    placing = (wanted[:, :, None] == local_ids[None, None, :]).astype(jnp.bfloat16)
    feature_grad = jnp.einsum(
        "scb,scfi->bif", placing, received, preferred_element_type=jnp.float32
    ).reshape(local_rows, col_width)
    return (activated.astype(jnp.bfloat16), weight_grad, feature_grad.astype(jnp.bfloat16))


def solution(mesh):
    return jax.shard_map(
        per_device,
        mesh=mesh,
        in_specs=(
            P("rows", "cols"),
            P(),
            P("rows", None, None),
            P("rows"),
            P("rows", None),
            P("rows"),
            P("rows"),
        ),
        out_specs=(P("rows", "cols"), P(None, "cols"), P("rows", "cols")),
        check_vma=False,
    )
```

```python
import math

import jax
import jax.numpy as jnp
from jax import lax
from jax.experimental import pallas as pl
from jax.experimental.pallas import tpu as pltpu
from jax.sharding import PartitionSpec as P

MESH = pl.DeviceIdType.MESH


def _cols_gather_kernel(x_ref, o_ref, send_sems, recv_sems, pass_sems, take_sems):
    n = o_ref.shape[0]
    chips = n // 2
    me = lax.axis_index("cols")
    partner = me + 1 - 2 * lax.rem(me, 2)
    barrier = pltpu.get_barrier_semaphore()
    for k in range(1, chips):
        pl.semaphore_signal(
            barrier, 1, device_id={"cols": lax.rem(me + 2 * k, n)}, device_id_type=MESH
        )
    pl.semaphore_signal(barrier, 1, device_id={"cols": partner}, device_id_type=MESH)
    pl.semaphore_wait(barrier, chips)
    near = [
        pltpu.make_async_remote_copy(
            src_ref=x_ref, dst_ref=o_ref.at[me], send_sem=pass_sems.at[0],
            recv_sem=take_sems.at[0], device_id={"cols": partner}, device_id_type=MESH)
    ]
    near[0].start()
    order = [chips // 2] + [k for k in range(1, chips) if k != chips // 2]
    far = {}
    for k in order:
        out = pltpu.make_async_remote_copy(
            src_ref=x_ref, dst_ref=o_ref.at[me], send_sem=send_sems.at[k],
            recv_sem=recv_sems.at[k], device_id={"cols": lax.rem(me + 2 * k, n)},
            device_id_type=MESH)
        out.start()
        src = lax.rem(me + n - 2 * k, n)
        back = pltpu.make_async_remote_copy(
            src_ref=x_ref, dst_ref=o_ref.at[src], send_sem=send_sems.at[k],
            recv_sem=recv_sems.at[k], device_id={"cols": src}, device_id_type=MESH)
        far[k] = (out, back)
    o_ref[me] = x_ref[...]
    for k in range(1, chips):
        out, back = far[k]
        back.wait_recv()
        piece = lax.rem(me + n - 2 * k, n)
        hop = pltpu.make_async_remote_copy(
            src_ref=o_ref.at[piece], dst_ref=o_ref.at[piece], send_sem=pass_sems.at[k],
            recv_sem=take_sems.at[k], device_id={"cols": partner}, device_id_type=MESH)
        hop.start()
        near.append(hop)
    for k in range(chips):
        piece = lax.rem(partner + n - 2 * k, n)
        pltpu.make_async_remote_copy(
            src_ref=o_ref.at[piece], dst_ref=o_ref.at[piece], send_sem=pass_sems.at[k],
            recv_sem=take_sems.at[k], device_id={"cols": partner}, device_id_type=MESH
        ).wait_recv()
    for out, back in far.values():
        out.wait_send()
    for hop in near:
        hop.wait_send()


def cols_gather(x, collective_id):
    n = lax.axis_size("cols")
    return pl.pallas_call(
        _cols_gather_kernel,
        out_shape=jax.ShapeDtypeStruct((n,) + x.shape, x.dtype),
        in_specs=[pl.BlockSpec(memory_space=pltpu.VMEM)],
        out_specs=pl.BlockSpec(memory_space=pltpu.VMEM),
        scratch_shapes=[pltpu.SemaphoreType.DMA((n,))] * 4,
        compiler_params=pltpu.CompilerParams(collective_id=collective_id, has_side_effects=True),
    )(x)


def slot_ranks(owners):
    positions = jnp.arange(owners.shape[0], dtype=jnp.int32)
    earlier = (owners[:, None] == owners[None, :]) & (positions[None, :] < positions[:, None])
    return jnp.sum(earlier.astype(jnp.int32), axis=1)


def rows_exchange(x):
    return lax.all_to_all(x, "rows", split_axis=0, concat_axis=0, tiled=True)


def per_device(node_features, weight, tile_values, tile_row, source_owner, source_block, labels):
    local_rows, col_width = node_features.shape
    block_size = tile_values.shape[1]
    local_blocks = local_rows // block_size
    row_devices = lax.axis_size("rows")
    col_devices = lax.axis_size("cols")
    tiles = tile_values.shape[0]
    capacity = 2 * tiles // row_devices
    owners = source_owner[:, 0]
    slot_rank = slot_ranks(owners)
    local_ids = jnp.arange(local_blocks, dtype=jnp.int32)
    row_onehot = (tile_row[:, None] == local_ids[None, :]).astype(jnp.float32)
    in_slot = (owners[:, None, None] == jnp.arange(row_devices, dtype=jnp.int32)[None, :, None]) & (
        slot_rank[:, None, None] == jnp.arange(capacity, dtype=jnp.int32)[None, None, :]
    )
    request = jnp.sum(jnp.where(in_slot, source_block[:, None, None], 0), axis=0)
    wanted = rows_exchange(request)
    own_blocks = node_features.reshape(local_blocks, block_size, col_width)
    incoming = rows_exchange(own_blocks[wanted])
    source_rows = incoming[owners, slot_rank]
    products = jnp.einsum(
        "tij,tjf->tif", tile_values, source_rows, preferred_element_type=jnp.float32
    )
    summed = jnp.einsum("tb,tif->bif", row_onehot, products, precision=lax.Precision.HIGHEST)
    aggregated = summed.reshape(local_rows, col_width).astype(jnp.bfloat16)
    aggregated_all = cols_gather(aggregated.T, 2)
    col_index = lax.axis_index("cols")
    w_columns = lax.dynamic_slice_in_dim(weight, col_index * col_width, col_width, 1)
    w_rows = lax.dynamic_slice_in_dim(weight, col_index * col_width, col_width, 0)
    w_split = w_columns.reshape(col_devices, col_width, col_width)
    hidden = jnp.einsum("jfn,jfc->nc", aggregated_all, w_split, preferred_element_type=jnp.float32)
    sigmoid = jax.nn.sigmoid(hidden)
    activated = hidden * sigmoid
    slopes = sigmoid * (1.0 + hidden * (1.0 - sigmoid))
    feature_ids = col_index * col_width + jnp.arange(col_width, dtype=jnp.int32)
    target = (labels[:, None] == feature_ids[None, :]).astype(jnp.float32)
    out_grad = ((activated - target) * slopes).astype(jnp.bfloat16)
    grad_all = cols_gather(out_grad.T, 3)
    weight_terms = jnp.einsum(
        "jfn,nc->jfc", aggregated_all, out_grad, preferred_element_type=jnp.float32
    ).reshape(col_devices * col_width, col_width)
    pieces = weight_terms.reshape(row_devices, -1, col_width)
    reduced = jnp.sum(rows_exchange(pieces), axis=0)
    high = reduced.astype(jnp.bfloat16)
    low = (reduced - high.astype(jnp.float32)).astype(jnp.bfloat16)
    chunk = jnp.concatenate([high, low], axis=0).reshape(-1, block_size)
    agg_grad = jnp.einsum(
        "jcn,kjc->nk",
        grad_all,
        w_rows.reshape(col_width, col_devices, col_width),
        preferred_element_type=jnp.float32,
    ).astype(jnp.bfloat16)
    grad_rows = agg_grad.reshape(local_blocks, block_size, col_width)[tile_row]
    sent_terms = jnp.einsum(
        "tji,tjf->tfi", tile_values, grad_rows, preferred_element_type=jnp.float32
    ).astype(jnp.bfloat16)
    slot_pick = in_slot.astype(jnp.bfloat16)
    send_terms = jnp.einsum(
        "tos,tfi->osfi", slot_pick, sent_terms, preferred_element_type=jnp.float32
    ).astype(jnp.bfloat16)
    payload = jnp.concatenate(
        [
            send_terms.reshape(row_devices, capacity * col_width, block_size),
            jnp.broadcast_to(chunk[None], (row_devices,) + chunk.shape),
        ],
        axis=1,
    )
    arrived = rows_exchange(payload)
    received = arrived[:, : capacity * col_width].reshape(
        row_devices, capacity, col_width, block_size
    )
    parts = arrived[:, capacity * col_width :].reshape(row_devices, 2, -1, col_width)
    node_total = local_rows * row_devices
    weight_grad = (parts[:, 0].astype(jnp.float32) + parts[:, 1].astype(jnp.float32)).reshape(
        col_devices * col_width, col_width
    ) / math.sqrt(node_total)
    placing = (wanted[:, :, None] == local_ids[None, None, :]).astype(jnp.bfloat16)
    feature_grad = jnp.einsum(
        "scb,scfi->bif", placing, received, preferred_element_type=jnp.float32
    ).reshape(local_rows, col_width)
    return (activated.astype(jnp.bfloat16), weight_grad, feature_grad.astype(jnp.bfloat16))


def solution(mesh):
    return jax.shard_map(
        per_device,
        mesh=mesh,
        in_specs=(
            P("rows", "cols"),
            P(),
            P("rows", None, None),
            P("rows"),
            P("rows", None),
            P("rows"),
            P("rows"),
        ),
        out_specs=(P("rows", "cols"), P(None, "cols"), P("rows", "cols")),
        check_vma=False,
    )
```

```python
import math

import jax
import jax.numpy as jnp
from jax import lax
from jax.experimental import pallas as pl
from jax.experimental.pallas import tpu as pltpu
from jax.sharding import PartitionSpec as P

MESH = pl.DeviceIdType.MESH


def _cols_gather_kernel(x_ref, o_ref, send_sems, recv_sems, pass_sems, take_sems):
    n = o_ref.shape[0]
    chips = n // 2
    far_k = chips // 2
    me = lax.axis_index("cols")
    core = lax.rem(me, 2)
    partner = me + 1 - 2 * core
    barrier = pltpu.get_barrier_semaphore()
    for k in range(1, chips):
        pl.semaphore_signal(
            barrier, 1, device_id={"cols": lax.rem(me + 2 * k, n)}, device_id_type=MESH
        )
    pl.semaphore_signal(barrier, 1, device_id={"cols": partner}, device_id_type=MESH)
    pl.semaphore_wait(barrier, chips)

    def direct(k):
        return pltpu.make_async_remote_copy(
            src_ref=x_ref, dst_ref=o_ref.at[me], send_sem=send_sems.at[k],
            recv_sem=recv_sems.at[k], device_id={"cols": lax.rem(me + 2 * k, n)},
            device_id_type=MESH)

    def arrival(k):
        src = lax.rem(me + n - 2 * k, n)
        return pltpu.make_async_remote_copy(
            src_ref=x_ref, dst_ref=o_ref.at[src], send_sem=send_sems.at[k],
            recv_sem=recv_sems.at[k], device_id={"cols": src}, device_id_type=MESH)

    relay_from = lax.rem(me + 2, n)
    relay = pltpu.make_async_remote_copy(
        src_ref=o_ref.at[relay_from], dst_ref=o_ref.at[relay_from], send_sem=send_sems.at[far_k],
        recv_sem=recv_sems.at[far_k], device_id={"cols": lax.rem(me + n - 2, n)},
        device_id_type=MESH)
    near = [
        pltpu.make_async_remote_copy(
            src_ref=x_ref, dst_ref=o_ref.at[me], send_sem=pass_sems.at[0],
            recv_sem=take_sems.at[0], device_id={"cols": partner}, device_id_type=MESH)
    ]
    near[0].start()
    for k in range(1, chips):
        if k == far_k:
            @pl.when(core == 0)
            def _():
                direct(k).start()
        else:
            direct(k).start()
    o_ref[me] = x_ref[...]
    order = [chips - 1] + [k for k in range(1, chips - 1)]
    for k in order:
        arrival(k).wait_recv()
        if k == chips - 1:
            @pl.when(core == 1)
            def _():
                relay.start()
        piece = lax.rem(me + n - 2 * k, n)
        hop = pltpu.make_async_remote_copy(
            src_ref=o_ref.at[piece], dst_ref=o_ref.at[piece], send_sem=pass_sems.at[k],
            recv_sem=take_sems.at[k], device_id={"cols": partner}, device_id_type=MESH)
        hop.start()
        near.append(hop)
    for k in range(chips):
        piece = lax.rem(partner + n - 2 * k, n)
        pltpu.make_async_remote_copy(
            src_ref=o_ref.at[piece], dst_ref=o_ref.at[piece], send_sem=pass_sems.at[k],
            recv_sem=take_sems.at[k], device_id={"cols": partner}, device_id_type=MESH
        ).wait_recv()
    for k in range(1, chips):
        direct(k).wait_send()
    for hop in near:
        hop.wait_send()


def cols_gather(x, collective_id):
    n = lax.axis_size("cols")
    return pl.pallas_call(
        _cols_gather_kernel,
        out_shape=jax.ShapeDtypeStruct((n,) + x.shape, x.dtype),
        in_specs=[pl.BlockSpec(memory_space=pltpu.VMEM)],
        out_specs=pl.BlockSpec(memory_space=pltpu.VMEM),
        scratch_shapes=[pltpu.SemaphoreType.DMA((n,))] * 4,
        compiler_params=pltpu.CompilerParams(collective_id=collective_id, has_side_effects=True),
    )(x)


def slot_ranks(owners):
    positions = jnp.arange(owners.shape[0], dtype=jnp.int32)
    earlier = (owners[:, None] == owners[None, :]) & (positions[None, :] < positions[:, None])
    return jnp.sum(earlier.astype(jnp.int32), axis=1)


def rows_exchange(x):
    return lax.all_to_all(x, "rows", split_axis=0, concat_axis=0, tiled=True)


def per_device(node_features, weight, tile_values, tile_row, source_owner, source_block, labels):
    local_rows, col_width = node_features.shape
    block_size = tile_values.shape[1]
    local_blocks = local_rows // block_size
    row_devices = lax.axis_size("rows")
    col_devices = lax.axis_size("cols")
    tiles = tile_values.shape[0]
    capacity = 2 * tiles // row_devices
    owners = source_owner[:, 0]
    slot_rank = slot_ranks(owners)
    local_ids = jnp.arange(local_blocks, dtype=jnp.int32)
    row_onehot = (tile_row[:, None] == local_ids[None, :]).astype(jnp.float32)
    in_slot = (owners[:, None, None] == jnp.arange(row_devices, dtype=jnp.int32)[None, :, None]) & (
        slot_rank[:, None, None] == jnp.arange(capacity, dtype=jnp.int32)[None, None, :]
    )
    request = jnp.sum(jnp.where(in_slot, source_block[:, None, None], 0), axis=0)
    wanted = rows_exchange(request)
    own_blocks = node_features.reshape(local_blocks, block_size, col_width)
    incoming = rows_exchange(own_blocks[wanted])
    source_rows = incoming[owners, slot_rank]
    products = jnp.einsum(
        "tij,tjf->tif", tile_values, source_rows, preferred_element_type=jnp.float32
    )
    summed = jnp.einsum("tb,tif->bif", row_onehot, products, precision=lax.Precision.HIGHEST)
    aggregated = summed.reshape(local_rows, col_width).astype(jnp.bfloat16)
    aggregated_all = cols_gather(aggregated.T, 2)
    col_index = lax.axis_index("cols")
    w_columns = lax.dynamic_slice_in_dim(weight, col_index * col_width, col_width, 1)
    w_rows = lax.dynamic_slice_in_dim(weight, col_index * col_width, col_width, 0)
    w_split = w_columns.reshape(col_devices, col_width, col_width)
    hidden = jnp.einsum("jfn,jfc->nc", aggregated_all, w_split, preferred_element_type=jnp.float32)
    sigmoid = jax.nn.sigmoid(hidden)
    activated = hidden * sigmoid
    slopes = sigmoid * (1.0 + hidden * (1.0 - sigmoid))
    feature_ids = col_index * col_width + jnp.arange(col_width, dtype=jnp.int32)
    target = (labels[:, None] == feature_ids[None, :]).astype(jnp.float32)
    out_grad = ((activated - target) * slopes).astype(jnp.bfloat16)
    grad_all = cols_gather(out_grad.T, 3)
    weight_terms = jnp.einsum(
        "jfn,nc->jfc", aggregated_all, out_grad, preferred_element_type=jnp.float32
    ).reshape(col_devices * col_width, col_width)
    pieces = weight_terms.reshape(row_devices, -1, col_width)
    reduced = jnp.sum(rows_exchange(pieces), axis=0)
    high = reduced.astype(jnp.bfloat16)
    low = (reduced - high.astype(jnp.float32)).astype(jnp.bfloat16)
    chunk = jnp.concatenate([high, low], axis=0).reshape(-1, block_size)
    agg_grad = jnp.einsum(
        "jcn,kjc->nk",
        grad_all,
        w_rows.reshape(col_width, col_devices, col_width),
        preferred_element_type=jnp.float32,
    ).astype(jnp.bfloat16)
    grad_rows = agg_grad.reshape(local_blocks, block_size, col_width)[tile_row]
    sent_terms = jnp.einsum(
        "tji,tjf->tfi", tile_values, grad_rows, preferred_element_type=jnp.float32
    ).astype(jnp.bfloat16)
    slot_pick = in_slot.astype(jnp.bfloat16)
    send_terms = jnp.einsum(
        "tos,tfi->osfi", slot_pick, sent_terms, preferred_element_type=jnp.float32
    ).astype(jnp.bfloat16)
    payload = jnp.concatenate(
        [
            send_terms.reshape(row_devices, capacity * col_width, block_size),
            jnp.broadcast_to(chunk[None], (row_devices,) + chunk.shape),
        ],
        axis=1,
    )
    arrived = rows_exchange(payload)
    received = arrived[:, : capacity * col_width].reshape(
        row_devices, capacity, col_width, block_size
    )
    parts = arrived[:, capacity * col_width :].reshape(row_devices, 2, -1, col_width)
    node_total = local_rows * row_devices
    weight_grad = (parts[:, 0].astype(jnp.float32) + parts[:, 1].astype(jnp.float32)).reshape(
        col_devices * col_width, col_width
    ) / math.sqrt(node_total)
    placing = (wanted[:, :, None] == local_ids[None, None, :]).astype(jnp.bfloat16)
    feature_grad = jnp.einsum(
        "scb,scfi->bif", placing, received, preferred_element_type=jnp.float32
    ).reshape(local_rows, col_width)
    return (activated.astype(jnp.bfloat16), weight_grad, feature_grad.astype(jnp.bfloat16))


def solution(mesh):
    return jax.shard_map(
        per_device,
        mesh=mesh,
        in_specs=(
            P("rows", "cols"),
            P(),
            P("rows", None, None),
            P("rows"),
            P("rows", None),
            P("rows"),
            P("rows"),
        ),
        out_specs=(P("rows", "cols"), P(None, "cols"), P("rows", "cols")),
        check_vma=False,
    )
```

```python
import math

import jax
import jax.numpy as jnp
from jax import lax
from jax.experimental import pallas as pl
from jax.experimental.pallas import tpu as pltpu
from jax.sharding import PartitionSpec as P

MESH = pl.DeviceIdType.MESH


def _cols_gather_kernel(x_ref, o_ref, send_sems, recv_sems, pass_sems, take_sems):
    n = o_ref.shape[0]
    chips = n // 2
    far_k = chips // 2
    me = lax.axis_index("cols")
    core = lax.rem(me, 2)
    partner = me + 1 - 2 * core
    barrier = pltpu.get_barrier_semaphore()
    for k in range(1, chips):
        pl.semaphore_signal(
            barrier, 1, device_id={"cols": lax.rem(me + 2 * k, n)}, device_id_type=MESH
        )
    pl.semaphore_signal(barrier, 1, device_id={"cols": partner}, device_id_type=MESH)
    pl.semaphore_wait(barrier, chips)

    def direct(k):
        return pltpu.make_async_remote_copy(
            src_ref=x_ref, dst_ref=o_ref.at[me], send_sem=send_sems.at[k],
            recv_sem=recv_sems.at[k], device_id={"cols": lax.rem(me + 2 * k, n)},
            device_id_type=MESH)

    def arrival(k):
        src = lax.rem(me + n - 2 * k, n)
        return pltpu.make_async_remote_copy(
            src_ref=x_ref, dst_ref=o_ref.at[src], send_sem=send_sems.at[k],
            recv_sem=recv_sems.at[k], device_id={"cols": src}, device_id_type=MESH)

    relay_from = lax.rem(me + 2, n)
    relay = pltpu.make_async_remote_copy(
        src_ref=o_ref.at[relay_from], dst_ref=o_ref.at[relay_from], send_sem=send_sems.at[far_k],
        recv_sem=recv_sems.at[far_k], device_id={"cols": lax.rem(me + n - 2, n)},
        device_id_type=MESH)
    near = [
        pltpu.make_async_remote_copy(
            src_ref=x_ref, dst_ref=o_ref.at[me], send_sem=pass_sems.at[0],
            recv_sem=take_sems.at[0], device_id={"cols": partner}, device_id_type=MESH)
    ]
    near[0].start()
    for k in range(1, chips):
        if k == far_k:
            @pl.when(core == 0)
            def _():
                direct(k).start()
        else:
            direct(k).start()
    o_ref[me] = x_ref[...]
    order = [chips - 1] + [k for k in range(1, chips - 1)]
    for k in order:
        arrival(k).wait_recv()
        if k == chips - 1:
            @pl.when(core == 1)
            def _():
                relay.start()
        piece = lax.rem(me + n - 2 * k, n)
        hop = pltpu.make_async_remote_copy(
            src_ref=o_ref.at[piece], dst_ref=o_ref.at[piece], send_sem=pass_sems.at[k],
            recv_sem=take_sems.at[k], device_id={"cols": partner}, device_id_type=MESH)
        hop.start()
        near.append(hop)
    for k in range(chips):
        piece = lax.rem(partner + n - 2 * k, n)
        pltpu.make_async_remote_copy(
            src_ref=o_ref.at[piece], dst_ref=o_ref.at[piece], send_sem=pass_sems.at[k],
            recv_sem=take_sems.at[k], device_id={"cols": partner}, device_id_type=MESH
        ).wait_recv()
    for k in range(1, chips):
        direct(k).wait_send()
    for hop in near:
        hop.wait_send()


def cols_gather(x, collective_id):
    n = lax.axis_size("cols")
    return pl.pallas_call(
        _cols_gather_kernel,
        out_shape=jax.ShapeDtypeStruct((n,) + x.shape, x.dtype),
        in_specs=[pl.BlockSpec(memory_space=pltpu.VMEM)],
        out_specs=pl.BlockSpec(memory_space=pltpu.VMEM),
        scratch_shapes=[pltpu.SemaphoreType.DMA((n,))] * 4,
        compiler_params=pltpu.CompilerParams(collective_id=collective_id, has_side_effects=True),
    )(x)


def slot_ranks(owners):
    positions = jnp.arange(owners.shape[0], dtype=jnp.int32)
    earlier = (owners[:, None] == owners[None, :]) & (positions[None, :] < positions[:, None])
    return jnp.sum(earlier.astype(jnp.int32), axis=1)


def rows_exchange(x):
    return lax.all_to_all(x, "rows", split_axis=0, concat_axis=0, tiled=True)


def per_device(node_features, weight, tile_values, tile_row, source_owner, source_block, labels):
    local_rows, col_width = node_features.shape
    block_size = tile_values.shape[1]
    local_blocks = local_rows // block_size
    row_devices = lax.axis_size("rows")
    col_devices = lax.axis_size("cols")
    tiles = tile_values.shape[0]
    capacity = 2 * tiles // row_devices
    owners = source_owner[:, 0]
    slot_rank = slot_ranks(owners)
    local_ids = jnp.arange(local_blocks, dtype=jnp.int32)
    row_onehot = (tile_row[:, None] == local_ids[None, :]).astype(jnp.float32)
    in_slot = (owners[:, None, None] == jnp.arange(row_devices, dtype=jnp.int32)[None, :, None]) & (
        slot_rank[:, None, None] == jnp.arange(capacity, dtype=jnp.int32)[None, None, :]
    )
    request = jnp.sum(jnp.where(in_slot, source_block[:, None, None], 0), axis=0)
    wanted = rows_exchange(request)
    own_blocks = node_features.reshape(local_blocks, block_size, col_width)
    incoming = rows_exchange(own_blocks[wanted])
    source_rows = incoming[owners, slot_rank]
    products = jnp.einsum(
        "tij,tjf->tif", tile_values, source_rows, preferred_element_type=jnp.float32
    )
    summed = jnp.einsum("tb,tif->bif", row_onehot, products, precision=lax.Precision.HIGHEST)
    aggregated = summed.reshape(local_rows, col_width).astype(jnp.bfloat16)
    aggregated_all = cols_gather(aggregated.T, 2)
    col_index = lax.axis_index("cols")
    w_columns = lax.dynamic_slice_in_dim(weight, col_index * col_width, col_width, 1)
    w_rows = lax.dynamic_slice_in_dim(weight, col_index * col_width, col_width, 0)
    w_split = w_columns.reshape(col_devices, col_width, col_width)
    hidden = jnp.einsum("jfn,jfc->nc", aggregated_all, w_split, preferred_element_type=jnp.float32)
    sigmoid = jax.nn.sigmoid(hidden)
    activated = hidden * sigmoid
    slopes = sigmoid * (1.0 + hidden * (1.0 - sigmoid))
    feature_ids = col_index * col_width + jnp.arange(col_width, dtype=jnp.int32)
    target = (labels[:, None] == feature_ids[None, :]).astype(jnp.float32)
    out_grad = ((activated - target) * slopes).astype(jnp.bfloat16)
    grad_all = cols_gather(out_grad.T, 3)
    weight_terms = jnp.einsum(
        "jfn,nc->jfc", aggregated_all, out_grad, preferred_element_type=jnp.float32
    ).reshape(col_devices * col_width, col_width)
    pieces = weight_terms.reshape(row_devices, -1, col_width)
    reduced = jnp.sum(rows_exchange(pieces), axis=0)
    high = reduced.astype(jnp.bfloat16)
    low = (reduced - high.astype(jnp.float32)).astype(jnp.bfloat16)
    chunk = jnp.concatenate([high, low], axis=0).reshape(-1, block_size)
    agg_grad = jnp.einsum(
        "jcn,kjc->nk",
        grad_all,
        w_rows.reshape(col_width, col_devices, col_width),
        preferred_element_type=jnp.float32,
    ).astype(jnp.bfloat16)
    grad_rows = agg_grad.reshape(local_blocks, block_size, col_width)[tile_row]
    sent_terms = jnp.einsum(
        "tji,tjf->tfi", tile_values, grad_rows, preferred_element_type=jnp.float32
    ).astype(jnp.bfloat16)
    slot_pick = in_slot.astype(jnp.bfloat16)
    send_terms = jnp.dot(
        jnp.transpose(slot_pick, (1, 2, 0)).reshape(row_devices * capacity, tiles),
        sent_terms.reshape(tiles, col_width * block_size),
        preferred_element_type=jnp.float32,
    ).astype(jnp.bfloat16)
    payload = jnp.concatenate(
        [
            send_terms.reshape(row_devices, capacity * col_width, block_size),
            jnp.broadcast_to(chunk[None], (row_devices,) + chunk.shape),
        ],
        axis=1,
    )
    arrived = rows_exchange(payload)
    received = arrived[:, : capacity * col_width].reshape(
        row_devices, capacity, col_width, block_size
    )
    parts = arrived[:, capacity * col_width :].reshape(row_devices, 2, -1, col_width)
    node_total = local_rows * row_devices
    weight_grad = (parts[:, 0].astype(jnp.float32) + parts[:, 1].astype(jnp.float32)).reshape(
        col_devices * col_width, col_width
    ) / math.sqrt(node_total)
    placing = (wanted[:, :, None] == local_ids[None, None, :]).astype(jnp.bfloat16)
    feature_grad = jnp.einsum(
        "scb,scfi->bif", placing, received, preferred_element_type=jnp.float32
    ).reshape(local_rows, col_width)
    return (activated.astype(jnp.bfloat16), weight_grad, feature_grad.astype(jnp.bfloat16))


def solution(mesh):
    return jax.shard_map(
        per_device,
        mesh=mesh,
        in_specs=(
            P("rows", "cols"),
            P(),
            P("rows", None, None),
            P("rows"),
            P("rows", None),
            P("rows"),
            P("rows"),
        ),
        out_specs=(P("rows", "cols"), P(None, "cols"), P("rows", "cols")),
        check_vma=False,
    )
```

```python
import math

import jax
import jax.numpy as jnp
from jax import lax
from jax.experimental import pallas as pl
from jax.experimental.pallas import tpu as pltpu
from jax.sharding import PartitionSpec as P

MESH = pl.DeviceIdType.MESH


def _cols_gather_kernel(x_ref, o_ref, send_sems, recv_sems, pass_sems, take_sems):
    n = o_ref.shape[0]
    chips = n // 2
    far_k = chips // 2
    me = lax.axis_index("cols")
    core = lax.rem(me, 2)
    partner = me + 1 - 2 * core
    barrier = pltpu.get_barrier_semaphore()
    for k in range(1, chips):
        pl.semaphore_signal(
            barrier, 1, device_id={"cols": lax.rem(me + 2 * k, n)}, device_id_type=MESH
        )
    pl.semaphore_signal(barrier, 1, device_id={"cols": partner}, device_id_type=MESH)
    pl.semaphore_wait(barrier, chips)

    def direct(k):
        return pltpu.make_async_remote_copy(
            src_ref=x_ref, dst_ref=o_ref.at[me], send_sem=send_sems.at[k],
            recv_sem=recv_sems.at[k], device_id={"cols": lax.rem(me + 2 * k, n)},
            device_id_type=MESH)

    def arrival(k):
        src = lax.rem(me + n - 2 * k, n)
        return pltpu.make_async_remote_copy(
            src_ref=x_ref, dst_ref=o_ref.at[src], send_sem=send_sems.at[k],
            recv_sem=recv_sems.at[k], device_id={"cols": src}, device_id_type=MESH)

    relay_from = lax.rem(me + 2, n)
    relay = pltpu.make_async_remote_copy(
        src_ref=o_ref.at[relay_from], dst_ref=o_ref.at[relay_from], send_sem=send_sems.at[far_k],
        recv_sem=recv_sems.at[far_k], device_id={"cols": lax.rem(me + n - 2, n)},
        device_id_type=MESH)
    near = [
        pltpu.make_async_remote_copy(
            src_ref=x_ref, dst_ref=o_ref.at[me], send_sem=pass_sems.at[0],
            recv_sem=take_sems.at[0], device_id={"cols": partner}, device_id_type=MESH)
    ]
    near[0].start()
    for k in range(1, chips):
        if k == far_k:
            @pl.when(core == 0)
            def _():
                direct(k).start()
        else:
            direct(k).start()
    o_ref[me] = x_ref[...]
    order = [chips - 1] + [k for k in range(1, chips - 1)]
    for k in order:
        arrival(k).wait_recv()
        if k == chips - 1:
            @pl.when(core == 1)
            def _():
                relay.start()
        piece = lax.rem(me + n - 2 * k, n)
        hop = pltpu.make_async_remote_copy(
            src_ref=o_ref.at[piece], dst_ref=o_ref.at[piece], send_sem=pass_sems.at[k],
            recv_sem=take_sems.at[k], device_id={"cols": partner}, device_id_type=MESH)
        hop.start()
        near.append(hop)
    for k in range(chips):
        piece = lax.rem(partner + n - 2 * k, n)
        pltpu.make_async_remote_copy(
            src_ref=o_ref.at[piece], dst_ref=o_ref.at[piece], send_sem=pass_sems.at[k],
            recv_sem=take_sems.at[k], device_id={"cols": partner}, device_id_type=MESH
        ).wait_recv()
    for k in range(1, chips):
        direct(k).wait_send()
    for hop in near:
        hop.wait_send()


def cols_gather(x, collective_id):
    n = lax.axis_size("cols")
    return pl.pallas_call(
        _cols_gather_kernel,
        out_shape=jax.ShapeDtypeStruct((n,) + x.shape, x.dtype),
        in_specs=[pl.BlockSpec(memory_space=pltpu.VMEM)],
        out_specs=pl.BlockSpec(memory_space=pltpu.VMEM),
        scratch_shapes=[pltpu.SemaphoreType.DMA((n,))] * 4,
        compiler_params=pltpu.CompilerParams(collective_id=collective_id, has_side_effects=True),
    )(x)


def slot_ranks(owners):
    positions = jnp.arange(owners.shape[0], dtype=jnp.int32)
    earlier = (owners[:, None] == owners[None, :]) & (positions[None, :] < positions[:, None])
    return jnp.sum(earlier.astype(jnp.int32), axis=1)


def rows_exchange(x):
    return lax.all_to_all(x, "rows", split_axis=0, concat_axis=0, tiled=True)


def per_device(node_features, weight, tile_values, tile_row, source_owner, source_block, labels):
    local_rows, col_width = node_features.shape
    block_size = tile_values.shape[1]
    local_blocks = local_rows // block_size
    row_devices = lax.axis_size("rows")
    col_devices = lax.axis_size("cols")
    tiles = tile_values.shape[0]
    capacity = 2 * tiles // row_devices
    owners = source_owner[:, 0]
    slot_rank = slot_ranks(owners)
    local_ids = jnp.arange(local_blocks, dtype=jnp.int32)
    row_onehot = (tile_row[:, None] == local_ids[None, :]).astype(jnp.float32)
    in_slot = (owners[:, None, None] == jnp.arange(row_devices, dtype=jnp.int32)[None, :, None]) & (
        slot_rank[:, None, None] == jnp.arange(capacity, dtype=jnp.int32)[None, None, :]
    )
    request = jnp.sum(jnp.where(in_slot, source_block[:, None, None], 0), axis=0)
    wanted = rows_exchange(request)
    own_blocks = node_features.reshape(local_blocks, block_size, col_width)
    incoming = rows_exchange(own_blocks[wanted])
    source_rows = incoming[owners, slot_rank]
    products = jnp.einsum(
        "tij,tjf->tif", tile_values, source_rows, preferred_element_type=jnp.float32
    )
    summed = jnp.einsum("tb,tif->bif", row_onehot, products, precision=lax.Precision.HIGH)
    aggregated = summed.reshape(local_rows, col_width).astype(jnp.bfloat16)
    aggregated_all = cols_gather(aggregated.T, 2)
    col_index = lax.axis_index("cols")
    w_columns = lax.dynamic_slice_in_dim(weight, col_index * col_width, col_width, 1)
    w_rows = lax.dynamic_slice_in_dim(weight, col_index * col_width, col_width, 0)
    w_split = w_columns.reshape(col_devices, col_width, col_width)
    hidden = jnp.einsum("jfn,jfc->nc", aggregated_all, w_split, preferred_element_type=jnp.float32)
    sigmoid = jax.nn.sigmoid(hidden)
    activated = hidden * sigmoid
    slopes = sigmoid * (1.0 + hidden * (1.0 - sigmoid))
    feature_ids = col_index * col_width + jnp.arange(col_width, dtype=jnp.int32)
    target = (labels[:, None] == feature_ids[None, :]).astype(jnp.float32)
    out_grad = ((activated - target) * slopes).astype(jnp.bfloat16)
    grad_all = cols_gather(out_grad.T, 3)
    weight_terms = jnp.einsum(
        "jfn,nc->jfc", aggregated_all, out_grad, preferred_element_type=jnp.float32
    ).reshape(col_devices * col_width, col_width)
    pieces = weight_terms.reshape(row_devices, -1, col_width)
    reduced = jnp.sum(rows_exchange(pieces), axis=0)
    high = reduced.astype(jnp.bfloat16)
    low = (reduced - high.astype(jnp.float32)).astype(jnp.bfloat16)
    chunk = jnp.concatenate([high, low], axis=0).reshape(-1, block_size)
    agg_grad = jnp.einsum(
        "jcn,kjc->nk",
        grad_all,
        w_rows.reshape(col_width, col_devices, col_width),
        preferred_element_type=jnp.float32,
    ).astype(jnp.bfloat16)
    grad_rows = agg_grad.reshape(local_blocks, block_size, col_width)[tile_row]
    sent_terms = jnp.einsum(
        "tji,tjf->tfi", tile_values, grad_rows, preferred_element_type=jnp.float32
    ).astype(jnp.bfloat16)
    slot_pick = in_slot.astype(jnp.bfloat16)
    send_terms = jnp.einsum(
        "tos,tfi->osfi", slot_pick, sent_terms, preferred_element_type=jnp.float32
    ).astype(jnp.bfloat16)
    payload = jnp.concatenate(
        [
            send_terms.reshape(row_devices, capacity * col_width, block_size),
            jnp.broadcast_to(chunk[None], (row_devices,) + chunk.shape),
        ],
        axis=1,
    )
    arrived = rows_exchange(payload)
    received = arrived[:, : capacity * col_width].reshape(
        row_devices, capacity, col_width, block_size
    )
    parts = arrived[:, capacity * col_width :].reshape(row_devices, 2, -1, col_width)
    node_total = local_rows * row_devices
    weight_grad = (parts[:, 0].astype(jnp.float32) + parts[:, 1].astype(jnp.float32)).reshape(
        col_devices * col_width, col_width
    ) / math.sqrt(node_total)
    placing = (wanted[:, :, None] == local_ids[None, None, :]).astype(jnp.bfloat16)
    feature_grad = jnp.einsum(
        "scb,scfi->bif", placing, received, preferred_element_type=jnp.float32
    ).reshape(local_rows, col_width)
    return (activated.astype(jnp.bfloat16), weight_grad, feature_grad.astype(jnp.bfloat16))


def solution(mesh):
    return jax.shard_map(
        per_device,
        mesh=mesh,
        in_specs=(
            P("rows", "cols"),
            P(),
            P("rows", None, None),
            P("rows"),
            P("rows", None),
            P("rows"),
            P("rows"),
        ),
        out_specs=(P("rows", "cols"), P(None, "cols"), P("rows", "cols")),
        check_vma=False,
    )
```
